128 devices in a mesh: fact: 8 (over x, core), dim: 16 (over z, y).
Axes of the slice: x: 4, y: 4, z: 4, core: 2. Of those that a mesh axis runs over, the one named last changes fastest.
Arguments:
- queries: bfloat16 [32768, 1024], P(('fact', 'dim')), may hold values from -6 to 6
- key_rows: bfloat16 [16384, 1024], P('dim'), may hold values from -6 to 6
- value_rows: bfloat16 [16384, 1024], P('dim'), may hold values from -6 to 6
- cotangent: bfloat16 [32768, 1024], P(('fact', 'dim')), may hold values from -6 to 6
- block_lists: int32 [256, 8], P(('fact', 'dim')), may hold values from 0 to 127, as said below
- tile_lengths: int32 [256], P(('fact', 'dim')), may hold values from 1 to 8, as said below
Outputs:
- attended: bfloat16 [32768, 1024], P(('fact', 'dim'))
- query_grad: bfloat16 [32768, 1024], P(('fact', 'dim'))
- key_grad: bfloat16 [16384, 1024], P('dim', 'fact')
- value_grad: bfloat16 [16384, 1024], P('dim', 'fact')
The draws below stay inside these ranges and needn't reach their ends.
Inputs may be any that keep to these rules, and one draw needn't show every extreme that they name: Rows of block_lists come in aligned groups of 2 rows. The entries of one row lie in different ranges [o * 8, (o + 1) * 8). Within one group, all entries that lie in one such range are the same block. Within each aligned run of 16 groups, the first entries of all rows lie in one common range. Only the first tile_lengths[t] entries of row t of block_lists are used.
All inputs are finite; a program needn't handle non-finite values.
Results may differ from the reference program's by a relative error of at most 0.0056.
Values may be sent and summed in bfloat16 or wider, within the bound.
A program may use at most 192 MiB of HBM per device.

```python
import math
import jax
import jax.numpy as jnp
from jax import lax

D = 1024
HEADS = 16
HEAD_DIM = 64
TILE = 128
LMAX = 8
TILES_DEV = 2
BLK_DEV = 8
NTILES = 256
FACTS = 32768
NBLK = 128
DROWS = 16384
N_FACT = 8
N_DIM = 16


def row_scales(key, row_count):
    return jnp.exp(jax.random.uniform(key, (row_count, 1), minval=math.log(0.3), maxval=math.log(3.0)))


def draw_queries(key, part):
    scales = row_scales(jax.random.fold_in(key, 2), FACTS)
    base_draw = jax.random.normal(jax.random.fold_in(key, 1), (FACTS, D)) * scales
    return jnp.clip(base_draw, -6.0, 6.0).astype(jnp.bfloat16)


def draw_key_rows(key, part):
    scales = row_scales(jax.random.fold_in(key, 4), DROWS)
    base_draw = jax.random.normal(jax.random.fold_in(key, 3), (DROWS, D)) * scales
    return jnp.clip(base_draw, -6.0, 6.0).astype(jnp.bfloat16)


def draw_block_lists(key, part):
    key_first, key_second, key_third = jax.random.split(jax.random.fold_in(key, 11), 3)
    device_total = N_FACT * N_DIM
    picked = jax.random.randint(key_first, (device_total, N_DIM), 0, BLK_DEV)
    hottest = jax.random.randint(key_second, (N_FACT,), 0, N_DIM)
    hot_device = jnp.repeat(hottest, N_DIM)
    device_of_tile = jnp.arange(NTILES, dtype=jnp.int32) // TILES_DEV
    owner_ids = jnp.arange(N_DIM, dtype=jnp.int32)
    rank_scores = jax.random.randint(key_third, (NTILES, N_DIM), 0, 65536) * N_DIM + owner_ids[None, :]
    rank_scores = jnp.where(owner_ids[None, :] == hot_device[device_of_tile][:, None], -1, rank_scores)
    owner_order = jnp.argsort(rank_scores, axis=1)[:, :LMAX].astype(jnp.int32)
    local_pick = jnp.take_along_axis(picked[device_of_tile], owner_order, axis=1)
    return (owner_order * BLK_DEV + local_pick).astype(jnp.int32)


def draw_tile_lengths(key, part):
    key_first, key_second, key_third = jax.random.split(jax.random.fold_in(key, 23), 3)
    device_caps = jax.random.randint(key_first, (N_FACT * N_DIM,), 1, LMAX + 1)
    device_of_tile = jnp.arange(NTILES, dtype=jnp.int32) // TILES_DEV
    raw_draws = jax.random.randint(key_second, (NTILES,), 0, 65536)
    lengths = 1 + raw_draws % device_caps[device_of_tile]
    forced = jax.random.randint(key_third, (), 0, NTILES)
    return lengths.at[forced].set(LMAX).astype(jnp.int32)


def level_of(key, extent, shards, low, high):
    gain = 1.0
    for dim, parts in shards:
        draws = jax.random.uniform(jax.random.fold_in(jax.random.fold_in(key, 6), dim), (parts,), jnp.float32, low / len(shards), high / len(shards))
        gain = gain * jnp.repeat(jnp.exp(draws), extent[dim] // parts).reshape((-1,) + (1,) * (len(extent) - 1 - dim))
    return gain


def scatter_about(rng, dims, width, reach, cuts=(), kind=jnp.bfloat16):
    values = jax.random.normal(rng, dims, jnp.float32) * width
    if len(cuts) > 0:
        values = level_of(rng, dims, cuts, -0.22, 0.18) * values
    return jnp.clip(values, min=-reach, max=reach).astype(kind)


def setup_inputs(seed: int = 0) -> dict:
    key_of = jax.random.split(jax.random.key(seed), 7)
    queries = draw_queries(jax.random.fold_in(key_of[6], 71), 0)
    key_rows = draw_key_rows(jax.random.fold_in(key_of[6], 71), 0)
    value_rows = scatter_about(key_of[2], (DROWS, D), 1.0, 6.0, ((0, 16),))
    cotangent = scatter_about(key_of[3], (FACTS, D), 1.0, 6.0, ((0, 128),))
    block_lists = draw_block_lists(jax.random.fold_in(key_of[6], 71), 0)
    tile_lengths = draw_tile_lengths(jax.random.fold_in(key_of[6], 71), 0)
    return {"queries": queries, "key_rows": key_rows, "value_rows": value_rows, "cotangent": cotangent, "block_lists": block_lists, "tile_lengths": tile_lengths}


NEG_FILL = -1e30


def reference(queries, key_rows, value_rows, cotangent, block_lists, tile_lengths):
    model_width = queries.shape[1]
    tile_count = queries.shape[0] // TILE
    slot_count = block_lists.shape[1]
    scale = HEAD_DIM ** -0.5
    gathered_key_blocks = key_rows.reshape(NBLK, TILE, model_width)
    gathered_value_blocks = value_rows.reshape(NBLK, TILE, model_width)
    query_tiles = queries.reshape(tile_count, TILE, HEADS, HEAD_DIM)
    grad_tiles = cotangent.reshape(tile_count, TILE, HEADS, HEAD_DIM)

    def one_tile(totals, inputs_step):
        key_total, value_total = totals
        query_one, grad_one, chosen, length = inputs_step
        chosen = chosen.astype(jnp.int32)
        key_one = gathered_key_blocks[chosen].reshape(slot_count * TILE, HEADS, HEAD_DIM).astype(jnp.float32)
        value_one = gathered_value_blocks[chosen].reshape(slot_count * TILE, HEADS, HEAD_DIM).astype(jnp.float32)
        alive_keys = (jnp.arange(slot_count * TILE, dtype=jnp.int32) // TILE) < length
        query_wide = query_one.astype(jnp.float32)
        grad_wide = grad_one.astype(jnp.float32)
        scores = jnp.einsum("qhe,khe->hqk", query_wide, key_one) * scale
        scores = jnp.where(alive_keys[None, None, :], scores, NEG_FILL)
        row_max = jnp.max(scores, axis=-1, keepdims=True)
        expo_terms = jnp.exp(scores - row_max)
        weights = expo_terms / jnp.sum(expo_terms, axis=-1, keepdims=True)
        weights_low = lax.optimization_barrier(weights.astype(jnp.bfloat16)).astype(jnp.float32)
        attended = jnp.einsum("hqk,khe->qhe", weights_low, value_one).astype(jnp.bfloat16)
        dweights = jnp.einsum("qhe,khe->hqk", grad_wide, value_one)
        row_delta = jnp.sum(weights * dweights, axis=-1, keepdims=True)
        dscores = lax.optimization_barrier((weights * (dweights - row_delta)).astype(jnp.bfloat16)).astype(jnp.float32)
        query_grad = (jnp.einsum("hqk,khe->qhe", dscores, key_one) * scale).astype(jnp.bfloat16)
        key_grad = jnp.einsum("hqk,qhe->khe", dscores, query_wide) * scale
        value_grad = jnp.einsum("hqk,qhe->khe", weights_low, grad_wide)
        key_total = key_total.at[chosen].add(key_grad.reshape(slot_count, TILE, model_width))
        value_total = value_total.at[chosen].add(value_grad.reshape(slot_count, TILE, model_width))
        return (key_total, value_total), (attended.reshape(TILE, model_width), query_grad.reshape(TILE, model_width))

    empty_total = jnp.zeros((NBLK, TILE, model_width), jnp.float32)
    (key_total, value_total), (attended, query_grad) = lax.scan(
        one_tile, (empty_total, empty_total), (query_tiles, grad_tiles, block_lists, tile_lengths))
    return (attended.reshape(FACTS, model_width),
            query_grad.reshape(FACTS, model_width),
            key_total.reshape(DROWS, model_width).astype(jnp.bfloat16),
            value_total.reshape(DROWS, model_width).astype(jnp.bfloat16))
```

```python
import jax
import jax.numpy as jnp
from jax import lax
from jax.sharding import PartitionSpec as P

HEADS = 16
HEAD_DIM = 64
TILE = 128


NEG_FILL = -1e30


def attend_group(query_group, grad_group, key_group, value_group, alive_keys):
    scale = HEAD_DIM ** (-0.5)
    scores = (
        jnp.einsum("tqhe,tkhe->thqk", query_group, key_group, preferred_element_type=jnp.float32)
        * scale
    )
    scores = jnp.where(alive_keys[:, None, None, :], scores, NEG_FILL)
    row_max = jnp.max(scores, axis=-1, keepdims=True)
    expo_terms = jnp.exp(scores - row_max)
    weights = expo_terms / jnp.sum(expo_terms, axis=-1, keepdims=True)
    weights_low = weights.astype(jnp.bfloat16)
    attended = jnp.einsum(
        "thqk,tkhe->tqhe", weights_low, value_group, preferred_element_type=jnp.float32
    )
    dweights = jnp.einsum(
        "tqhe,tkhe->thqk", grad_group, value_group, preferred_element_type=jnp.float32
    )
    row_delta = jnp.sum(weights * dweights, axis=-1, keepdims=True)
    dscores = (weights * (dweights - row_delta)).astype(jnp.bfloat16)
    query_grad = (
        jnp.einsum("thqk,tkhe->tqhe", dscores, key_group, preferred_element_type=jnp.float32)
        * scale
    )
    key_grad = (
        jnp.einsum("thqk,tqhe->tkhe", dscores, query_group, preferred_element_type=jnp.float32)
        * scale
    )
    value_grad = jnp.einsum(
        "thqk,tqhe->tkhe", weights_low, grad_group, preferred_element_type=jnp.float32
    )
    return (attended, query_grad, key_grad, value_grad)


def body(queries, key_rows, value_rows, cotangent, block_lists, tile_lengths):
    owners = lax.axis_size("dim")
    tile_count = block_lists.shape[0]
    slot_count = block_lists.shape[1]
    blocks_here = key_rows.shape[0] // TILE
    model_width = key_rows.shape[1]
    head_size = HEAD_DIM
    half_heads = HEADS // 2
    alive_slots = jnp.arange(slot_count, dtype=jnp.int32)[None, :] < tile_lengths[:, None]
    owner_of = block_lists // blocks_here
    local_of = block_lists % blocks_here
    owner_ids = jnp.arange(owners, dtype=jnp.int32)
    matched = (owner_of[:, :, None] == owner_ids[None, None, :]) & alive_slots[:, :, None]
    wanted = jnp.max(jnp.where(matched, local_of[:, :, None], -1), axis=(0, 1))
    requests = lax.all_to_all(
        wanted.reshape(owners, 1), "dim", split_axis=0, concat_axis=0, tiled=True
    )
    block_ids = jnp.arange(blocks_here, dtype=jnp.int32)[None, :]
    slot_selector = (requests == block_ids).astype(jnp.bfloat16)
    gathered_key_blocks = key_rows.reshape(blocks_here, TILE, model_width)
    gathered_value_blocks = value_rows.reshape(blocks_here, TILE, model_width)
    reply_keys = jnp.einsum(
        "nh,hcm->ncm", slot_selector, gathered_key_blocks, preferred_element_type=jnp.float32
    ).astype(jnp.bfloat16)
    reply_values = jnp.einsum(
        "nh,hcm->ncm", slot_selector, gathered_value_blocks, preferred_element_type=jnp.float32
    ).astype(jnp.bfloat16)
    fetched_keys, fetched_values = (
        lax.all_to_all(reply_keys, "dim", split_axis=0, concat_axis=0, tiled=True),
        lax.all_to_all(reply_values, "dim", split_axis=0, concat_axis=0, tiled=True),
    )
    per_step = min(4, tile_count)
    step_count = tile_count // per_step
    query_steps = queries.reshape(step_count, per_step, TILE, model_width)
    grad_steps = cotangent.reshape(step_count, per_step, TILE, model_width)
    owner_steps = owner_of.reshape(step_count, per_step, slot_count)
    alive_steps = alive_slots.reshape(step_count, per_step, slot_count)
    match_steps = matched.astype(jnp.float32).reshape(step_count, per_step, slot_count, owners)
    span = half_heads * head_size

    def one_group(totals, inputs_step):
        key_total, value_total = totals
        query_block, grad_block, owner_step, alive_step, match_step = inputs_step
        key_group = fetched_keys[owner_step]
        value_group = fetched_values[owner_step]
        alive_keys = jnp.repeat(alive_step, TILE, axis=1)
        attended_parts = []
        query_parts = []
        key_parts = []
        value_parts = []
        for portion in range(2):
            start = portion * span
            query_half = query_block[..., start : start + span].reshape(
                per_step, TILE, half_heads, head_size
            )
            grad_half = grad_block[..., start : start + span].reshape(
                per_step, TILE, half_heads, head_size
            )
            key_half = key_group[..., start : start + span].reshape(
                per_step, slot_count * TILE, half_heads, head_size
            )
            value_half = value_group[..., start : start + span].reshape(
                per_step, slot_count * TILE, half_heads, head_size
            )
            attended, query_grad, key_grad, value_grad = attend_group(
                query_half, grad_half, key_half, value_half, alive_keys
            )
            attended_parts.append(attended.reshape(per_step, TILE, span))
            query_parts.append(query_grad.reshape(per_step, TILE, span))
            key_parts.append(key_grad.reshape(per_step, slot_count, TILE, span))
            value_parts.append(value_grad.reshape(per_step, slot_count, TILE, span))
        key_full = jnp.concatenate(key_parts, axis=-1)
        value_full = jnp.concatenate(value_parts, axis=-1)
        key_total = key_total + jnp.einsum(
            "tjo,tjkd->okd", match_step, key_full, precision=lax.Precision.HIGHEST
        )
        value_total = value_total + jnp.einsum(
            "tjo,tjkd->okd", match_step, value_full, precision=lax.Precision.HIGHEST
        )
        attended_block = jnp.concatenate(attended_parts, axis=-1).astype(jnp.bfloat16)
        query_block_grad = jnp.concatenate(query_parts, axis=-1).astype(jnp.bfloat16)
        return ((key_total, value_total), (attended_block, query_block_grad))

    empty_total = jnp.zeros((owners, TILE, model_width), jnp.float32)
    (partial_keys, partial_values), (attended_all, query_grad_all) = lax.scan(
        one_group,
        (empty_total, empty_total),
        (query_steps, grad_steps, owner_steps, alive_steps, match_steps),
    )
    attended_out = attended_all.reshape(tile_count * TILE, model_width)
    query_grad_out = query_grad_all.reshape(tile_count * TILE, model_width)
    incoming_key_rows, incoming_value_rows = (
        lax.all_to_all(partial_keys.astype(jnp.bfloat16), "dim", split_axis=0, concat_axis=0, tiled=True),
        lax.all_to_all(partial_values.astype(jnp.bfloat16), "dim", split_axis=0, concat_axis=0, tiled=True),
    )
    incoming_key_rows = incoming_key_rows.astype(jnp.float32)
    incoming_value_rows = incoming_value_rows.astype(jnp.float32)
    block_selector = (requests == block_ids).astype(jnp.float32)
    reduced_key_grad = jnp.einsum(
        "ep,ejs->pjs", block_selector, incoming_key_rows, precision=lax.Precision.HIGHEST
    )
    summed_values = jnp.einsum(
        "ep,ejs->pjs", block_selector, incoming_value_rows, precision=lax.Precision.HIGHEST
    )
    key_grad_out, value_grad_out = (
        lax.psum_scatter(
            reduced_key_grad.reshape(blocks_here * TILE, model_width),
            "fact",
            scatter_dimension=1,
            tiled=True,
        ),
        lax.psum_scatter(
            summed_values.reshape(blocks_here * TILE, model_width),
            "fact",
            scatter_dimension=1,
            tiled=True,
        ),
    )
    return (
        attended_out,
        query_grad_out,
        key_grad_out.astype(jnp.bfloat16),
        value_grad_out.astype(jnp.bfloat16),
    )


def solution(mesh):
    in_specs = (
        P(("fact", "dim"), None),
        P("dim", None),
        P("dim", None),
        P(("fact", "dim"), None),
        P(("fact", "dim"), None),
        P(("fact", "dim")),
    )
    out_specs = (
        P(("fact", "dim"), None),
        P(("fact", "dim"), None),
        P("dim", "fact"),
        P("dim", "fact"),
    )
    return jax.shard_map(body, mesh=mesh, in_specs=in_specs, out_specs=out_specs, check_vma=False)
```

```python
import functools
import jax
import jax.numpy as jnp
from jax import lax
from jax.experimental import pallas as pl
from jax.experimental.pallas import tpu as pltpu
from jax.sharding import PartitionSpec as P

HEADS = 16
HEAD_DIM = 64
TILE = 128
NEG_FILL = -1e30
PAIR = 2 * HEAD_DIM


def _nt(a, b):
    return lax.dot_general(a, b, (((1,), (1,)), ((), ())), preferred_element_type=jnp.float32)


def _tn(a, b):
    return lax.dot_general(a, b, (((0,), (0,)), ((), ())), preferred_element_type=jnp.float32)


def _nn(a, b):
    return jnp.dot(a, b, preferred_element_type=jnp.float32)


def attention_kernel(owner_ref, length_ref, q_ref, g_ref, k_ref, v_ref,
                     att_ref, qg_ref, dk_ref, dv_ref, kbuf, vbuf):
    tiles = q_ref.shape[0] // TILE
    slots = kbuf.shape[0] // TILE
    scale = HEAD_DIM ** (-0.5)
    dk_ref[...] = jnp.zeros_like(dk_ref)
    dv_ref[...] = jnp.zeros_like(dv_ref)
    lane = lax.broadcasted_iota(jnp.int32, (1, PAIR), 1)
    first = lane < HEAD_DIM
    key_pos = lax.broadcasted_iota(jnp.int32, (1, slots * TILE), 1)
    for t in range(tiles):
        rows = pl.ds(t * TILE, TILE)
        for j in range(slots):
            owner = owner_ref[t, j]
            kbuf[pl.ds(j * TILE, TILE), :] = k_ref[owner]
            vbuf[pl.ds(j * TILE, TILE), :] = v_ref[owner]
        q = q_ref[rows, :]
        g = g_ref[rows, :]
        keys = kbuf[...]
        values = vbuf[...]
        alive = key_pos < length_ref[t] * TILE
        outs = []
        for h in range(2):
            mine = first if h == 0 else jnp.logical_not(first)
            qh = jnp.where(mine, q, jnp.zeros_like(q))
            gh = jnp.where(mine, g, jnp.zeros_like(g))
            scores = _nt(qh, keys) * scale
            scores = jnp.where(alive, scores, NEG_FILL)
            row_max = jnp.max(scores, axis=-1, keepdims=True)
            expo = jnp.exp(scores - row_max)
            weights = expo / jnp.sum(expo, axis=-1, keepdims=True)
            weights_low = weights.astype(jnp.bfloat16)
            attended = _nn(weights_low, values)
            dweights = _nt(gh, values)
            row_delta = jnp.sum(weights * dweights, axis=-1, keepdims=True)
            dscores = (weights * (dweights - row_delta)).astype(jnp.bfloat16)
            query_grad = _nn(dscores, keys)
            key_grad = _tn(dscores, q)
            value_grad = _tn(weights_low, g)
            outs.append((attended, query_grad, key_grad, value_grad))
        pick = lambda i: jnp.where(first, outs[0][i], outs[1][i])
        att_ref[rows, :] = pick(0).astype(att_ref.dtype)
        qg_ref[rows, :] = (pick(1) * scale).astype(qg_ref.dtype)
        key_grad = pick(2) * scale
        value_grad = pick(3)
        for j in range(slots):
            owner = owner_ref[t, j]
            dk_ref[owner] = dk_ref[owner] + key_grad[j * TILE:(j + 1) * TILE]
            dv_ref[owner] = dv_ref[owner] + value_grad[j * TILE:(j + 1) * TILE]


def attend_local(owner_of, tile_lengths, queries, cotangent, fetched_keys, fetched_values):
    owners, _, width = fetched_keys.shape
    rows = queries.shape[0]
    slots = owner_of.shape[1]
    pairs = width // PAIR
    col = lambda hp, own, ln: (0, hp)
    blk = lambda hp, own, ln: (0, 0, hp)
    grid_spec = pltpu.PrefetchScalarGridSpec(
        num_scalar_prefetch=2,
        grid=(pairs,),
        in_specs=[
            pl.BlockSpec((rows, PAIR), col),
            pl.BlockSpec((rows, PAIR), col),
            pl.BlockSpec((owners, TILE, PAIR), blk),
            pl.BlockSpec((owners, TILE, PAIR), blk),
        ],
        out_specs=[
            pl.BlockSpec((rows, PAIR), col),
            pl.BlockSpec((rows, PAIR), col),
            pl.BlockSpec((owners, TILE, PAIR), blk),
            pl.BlockSpec((owners, TILE, PAIR), blk),
        ],
        scratch_shapes=[
            pltpu.VMEM((slots * TILE, PAIR), jnp.bfloat16),
            pltpu.VMEM((slots * TILE, PAIR), jnp.bfloat16),
        ],
    )
    return pl.pallas_call(
        attention_kernel,
        grid_spec=grid_spec,
        out_shape=[
            jax.ShapeDtypeStruct((rows, width), jnp.bfloat16),
            jax.ShapeDtypeStruct((rows, width), jnp.bfloat16),
            jax.ShapeDtypeStruct((owners, TILE, width), jnp.float32),
            jax.ShapeDtypeStruct((owners, TILE, width), jnp.float32),
        ],
        compiler_params=pltpu.CompilerParams(dimension_semantics=("arbitrary",)),
    )(owner_of, tile_lengths, queries, cotangent, fetched_keys, fetched_values)


def body(queries, key_rows, value_rows, cotangent, block_lists, tile_lengths):
    owners = lax.axis_size("dim")
    tile_count = block_lists.shape[0]
    slot_count = block_lists.shape[1]
    blocks_here = key_rows.shape[0] // TILE
    model_width = key_rows.shape[1]
    alive_slots = jnp.arange(slot_count, dtype=jnp.int32)[None, :] < tile_lengths[:, None]
    owner_of = block_lists // blocks_here
    local_of = block_lists % blocks_here
    owner_ids = jnp.arange(owners, dtype=jnp.int32)
    matched = (owner_of[:, :, None] == owner_ids[None, None, :]) & alive_slots[:, :, None]
    wanted = jnp.max(jnp.where(matched, local_of[:, :, None], -1), axis=(0, 1))
    requests = lax.all_to_all(
        wanted.reshape(owners, 1), "dim", split_axis=0, concat_axis=0, tiled=True
    )
    block_ids = jnp.arange(blocks_here, dtype=jnp.int32)[None, :]
    slot_selector = (requests == block_ids).astype(jnp.bfloat16)
    gathered_key_blocks = key_rows.reshape(blocks_here, TILE, model_width)
    gathered_value_blocks = value_rows.reshape(blocks_here, TILE, model_width)
    reply_keys = jnp.einsum(
        "nh,hcm->ncm", slot_selector, gathered_key_blocks, preferred_element_type=jnp.float32
    ).astype(jnp.bfloat16)
    reply_values = jnp.einsum(
        "nh,hcm->ncm", slot_selector, gathered_value_blocks, preferred_element_type=jnp.float32
    ).astype(jnp.bfloat16)
    fetched_keys, fetched_values = (
        lax.all_to_all(reply_keys, "dim", split_axis=0, concat_axis=0, tiled=True),
        lax.all_to_all(reply_values, "dim", split_axis=0, concat_axis=0, tiled=True),
    )
    attended_out, query_grad_out, partial_keys, partial_values = attend_local(
        owner_of, tile_lengths, queries, cotangent, fetched_keys, fetched_values
    )
    incoming_key_rows, incoming_value_rows = (
        lax.all_to_all(partial_keys.astype(jnp.bfloat16), "dim", split_axis=0, concat_axis=0, tiled=True),
        lax.all_to_all(partial_values.astype(jnp.bfloat16), "dim", split_axis=0, concat_axis=0, tiled=True),
    )
    incoming_key_rows = incoming_key_rows.astype(jnp.float32)
    incoming_value_rows = incoming_value_rows.astype(jnp.float32)
    block_selector = (requests == block_ids).astype(jnp.float32)
    reduced_key_grad = jnp.einsum(
        "ep,ejs->pjs", block_selector, incoming_key_rows, precision=lax.Precision.HIGHEST
    )
    summed_values = jnp.einsum(
        "ep,ejs->pjs", block_selector, incoming_value_rows, precision=lax.Precision.HIGHEST
    )
    key_grad_out, value_grad_out = (
        lax.psum_scatter(
            reduced_key_grad.reshape(blocks_here * TILE, model_width),
            "fact",
            scatter_dimension=1,
            tiled=True,
        ),
        lax.psum_scatter(
            summed_values.reshape(blocks_here * TILE, model_width),
            "fact",
            scatter_dimension=1,
            tiled=True,
        ),
    )
    return (
        attended_out,
        query_grad_out,
        key_grad_out.astype(jnp.bfloat16),
        value_grad_out.astype(jnp.bfloat16),
    )


def solution(mesh):
    in_specs = (
        P(("fact", "dim"), None),
        P("dim", None),
        P("dim", None),
        P(("fact", "dim"), None),
        P(("fact", "dim"), None),
        P(("fact", "dim")),
    )
    out_specs = (
        P(("fact", "dim"), None),
        P(("fact", "dim"), None),
        P("dim", "fact"),
        P("dim", "fact"),
    )
    return jax.shard_map(body, mesh=mesh, in_specs=in_specs, out_specs=out_specs, check_vma=False)
```

```python
import functools
import jax
import jax.numpy as jnp
from jax import lax
from jax.experimental import pallas as pl
from jax.experimental.pallas import tpu as pltpu
from jax.sharding import PartitionSpec as P

HEADS = 16
HEAD_DIM = 64
TILE = 128
NEG_FILL = -1e30
PAIR = 2 * HEAD_DIM


def _nt(a, b):
    return lax.dot_general(a, b, (((1,), (1,)), ((), ())), preferred_element_type=jnp.float32)


def _tn(a, b):
    return lax.dot_general(a, b, (((0,), (0,)), ((), ())), preferred_element_type=jnp.float32)


def _nn(a, b):
    return jnp.dot(a, b, preferred_element_type=jnp.float32)


def attention_kernel(owner_ref, length_ref, q_ref, g_ref, k_ref, v_ref,
                     att_ref, qg_ref, dk_out, dv_out, kbuf, vbuf, dk_ref, dv_ref):
    tiles = q_ref.shape[0] // TILE
    slots = kbuf.shape[0] // TILE
    scale = HEAD_DIM ** (-0.5)
    dk_ref[...] = jnp.zeros_like(dk_ref)
    dv_ref[...] = jnp.zeros_like(dv_ref)
    lane = lax.broadcasted_iota(jnp.int32, (1, PAIR), 1)
    first = lane < HEAD_DIM
    key_pos = lax.broadcasted_iota(jnp.int32, (1, slots * TILE), 1)
    for t in range(tiles):
        rows = pl.ds(t * TILE, TILE)
        for j in range(slots):
            owner = owner_ref[t, j]
            kbuf[pl.ds(j * TILE, TILE), :] = k_ref[owner]
            vbuf[pl.ds(j * TILE, TILE), :] = v_ref[owner]
        q = q_ref[rows, :]
        g = g_ref[rows, :]
        keys = kbuf[...]
        values = vbuf[...]
        alive = key_pos < length_ref[t] * TILE
        outs = []
        for h in range(2):
            mine = first if h == 0 else jnp.logical_not(first)
            qh = jnp.where(mine, q, jnp.zeros_like(q))
            gh = jnp.where(mine, g, jnp.zeros_like(g))
            scores = _nt(qh, keys) * scale
            scores = jnp.where(alive, scores, NEG_FILL)
            row_max = jnp.max(scores, axis=-1, keepdims=True)
            expo = jnp.exp(scores - row_max)
            weights = expo / jnp.sum(expo, axis=-1, keepdims=True)
            weights_low = weights.astype(jnp.bfloat16)
            attended = _nn(weights_low, values)
            dweights = _nt(gh, values)
            row_delta = jnp.sum(weights * dweights, axis=-1, keepdims=True)
            dscores = (weights * (dweights - row_delta)).astype(jnp.bfloat16)
            query_grad = _nn(dscores, keys)
            key_grad = _tn(dscores, q)
            value_grad = _tn(weights_low, g)
            outs.append((attended, query_grad, key_grad, value_grad))
        pick = lambda i: jnp.where(first, outs[0][i], outs[1][i])
        att_ref[rows, :] = pick(0).astype(att_ref.dtype)
        qg_ref[rows, :] = (pick(1) * scale).astype(qg_ref.dtype)
        key_grad = pick(2) * scale
        value_grad = pick(3)
        for j in range(slots):
            owner = owner_ref[t, j]
            dk_ref[owner] = dk_ref[owner] + key_grad[j * TILE:(j + 1) * TILE]
            dv_ref[owner] = dv_ref[owner] + value_grad[j * TILE:(j + 1) * TILE]
    dk_out[0] = dk_ref[...].astype(dk_out.dtype)
    dv_out[0] = dv_ref[...].astype(dv_out.dtype)


def attend_local(owner_of, tile_lengths, queries, cotangent, fetched_keys, fetched_values):
    owners, _, width = fetched_keys.shape
    rows = queries.shape[0]
    slots = owner_of.shape[1]
    pairs = width // PAIR
    col = lambda hp, own, ln: (0, hp)
    blk = lambda hp, own, ln: (0, 0, hp)
    grid_spec = pltpu.PrefetchScalarGridSpec(
        num_scalar_prefetch=2,
        grid=(pairs,),
        in_specs=[
            pl.BlockSpec((rows, PAIR), col),
            pl.BlockSpec((rows, PAIR), col),
            pl.BlockSpec((owners, TILE, PAIR), blk),
            pl.BlockSpec((owners, TILE, PAIR), blk),
        ],
        out_specs=[
            pl.BlockSpec((rows, PAIR), col),
            pl.BlockSpec((rows, PAIR), col),
            pl.BlockSpec((1, owners, TILE, PAIR), lambda hp, own, ln: (hp, 0, 0, 0)),
            pl.BlockSpec((1, owners, TILE, PAIR), lambda hp, own, ln: (hp, 0, 0, 0)),
        ],
        scratch_shapes=[
            pltpu.VMEM((slots * TILE, PAIR), jnp.bfloat16),
            pltpu.VMEM((slots * TILE, PAIR), jnp.bfloat16),
            pltpu.VMEM((owners, TILE, PAIR), jnp.float32),
            pltpu.VMEM((owners, TILE, PAIR), jnp.float32),
        ],
    )
    return pl.pallas_call(
        attention_kernel,
        grid_spec=grid_spec,
        out_shape=[
            jax.ShapeDtypeStruct((rows, width), jnp.bfloat16),
            jax.ShapeDtypeStruct((rows, width), jnp.bfloat16),
            jax.ShapeDtypeStruct((pairs, owners, TILE, PAIR), jnp.bfloat16),
            jax.ShapeDtypeStruct((pairs, owners, TILE, PAIR), jnp.bfloat16),
        ],
        compiler_params=pltpu.CompilerParams(dimension_semantics=("arbitrary",)),
    )(owner_of, tile_lengths, queries, cotangent, fetched_keys, fetched_values)


def body(queries, key_rows, value_rows, cotangent, block_lists, tile_lengths):
    owners = lax.axis_size("dim")
    tile_count = block_lists.shape[0]
    slot_count = block_lists.shape[1]
    blocks_here = key_rows.shape[0] // TILE
    model_width = key_rows.shape[1]
    alive_slots = jnp.arange(slot_count, dtype=jnp.int32)[None, :] < tile_lengths[:, None]
    owner_of = block_lists // blocks_here
    local_of = block_lists % blocks_here
    owner_ids = jnp.arange(owners, dtype=jnp.int32)
    matched = (owner_of[:, :, None] == owner_ids[None, None, :]) & alive_slots[:, :, None]
    wanted = jnp.max(jnp.where(matched, local_of[:, :, None], -1), axis=(0, 1))
    requests = lax.all_to_all(
        wanted.reshape(owners, 1), "dim", split_axis=0, concat_axis=0, tiled=True
    )
    block_ids = jnp.arange(blocks_here, dtype=jnp.int32)[None, :]
    slot_selector = (requests == block_ids).astype(jnp.bfloat16)
    gathered_key_blocks = key_rows.reshape(blocks_here, TILE, model_width)
    gathered_value_blocks = value_rows.reshape(blocks_here, TILE, model_width)
    reply_keys = jnp.einsum(
        "nh,hcm->ncm", slot_selector, gathered_key_blocks, preferred_element_type=jnp.float32
    ).astype(jnp.bfloat16)
    reply_values = jnp.einsum(
        "nh,hcm->ncm", slot_selector, gathered_value_blocks, preferred_element_type=jnp.float32
    ).astype(jnp.bfloat16)
    fetched_keys, fetched_values = (
        lax.all_to_all(reply_keys, "dim", split_axis=0, concat_axis=0, tiled=True),
        lax.all_to_all(reply_values, "dim", split_axis=0, concat_axis=0, tiled=True),
    )
    attended_out, query_grad_out, partial_keys, partial_values = attend_local(
        owner_of, tile_lengths, queries, cotangent, fetched_keys, fetched_values
    )
    fact_count = lax.axis_size("fact")
    everyone = ("fact", "dim")
    pieces_keys = lax.all_to_all(
        partial_keys.reshape(fact_count * owners, TILE, model_width // fact_count),
        everyone, split_axis=0, concat_axis=0, tiled=True,
    )
    pieces_values = lax.all_to_all(
        partial_values.reshape(fact_count * owners, TILE, model_width // fact_count),
        everyone, split_axis=0, concat_axis=0, tiled=True,
    )
    all_requests = lax.all_gather(requests.reshape(owners), "fact", tiled=True)
    block_selector = (all_requests[:, None] == block_ids).astype(jnp.float32)
    key_grad_out = jnp.einsum(
        "ep,ejs->pjs", block_selector, pieces_keys.astype(jnp.float32),
        precision=lax.Precision.HIGHEST,
    ).reshape(blocks_here * TILE, model_width // fact_count)
    value_grad_out = jnp.einsum(
        "ep,ejs->pjs", block_selector, pieces_values.astype(jnp.float32),
        precision=lax.Precision.HIGHEST,
    ).reshape(blocks_here * TILE, model_width // fact_count)
    return (
        attended_out,
        query_grad_out,
        key_grad_out.astype(jnp.bfloat16),
        value_grad_out.astype(jnp.bfloat16),
    )


def solution(mesh):
    in_specs = (
        P(("fact", "dim"), None),
        P("dim", None),
        P("dim", None),
        P(("fact", "dim"), None),
        P(("fact", "dim"), None),
        P(("fact", "dim")),
    )
    out_specs = (
        P(("fact", "dim"), None),
        P(("fact", "dim"), None),
        P("dim", "fact"),
        P("dim", "fact"),
    )
    return jax.shard_map(body, mesh=mesh, in_specs=in_specs, out_specs=out_specs, check_vma=False)
```

```python
import functools
import jax
import jax.numpy as jnp
from jax import lax
from jax.experimental import pallas as pl
from jax.experimental.pallas import tpu as pltpu
from jax.sharding import PartitionSpec as P

HEADS = 16
HEAD_DIM = 64
TILE = 128
NEG_FILL = -1e30
PAIR = 2 * HEAD_DIM


def _nt(a, b):
    return lax.dot_general(a, b, (((1,), (1,)), ((), ())), preferred_element_type=jnp.float32)


def _tn(a, b):
    return lax.dot_general(a, b, (((0,), (0,)), ((), ())), preferred_element_type=jnp.float32)


def _nn(a, b):
    return jnp.dot(a, b, preferred_element_type=jnp.float32)


def attention_kernel(owner_ref, length_ref, q_ref, g_ref, k_ref, v_ref,
                     att_ref, qg_ref, grad_out, kbuf, vbuf, dk_ref, dv_ref):
    tiles = q_ref.shape[0] // TILE
    slots = kbuf.shape[0] // TILE
    scale = HEAD_DIM ** (-0.5)
    dk_ref[...] = jnp.zeros_like(dk_ref)
    dv_ref[...] = jnp.zeros_like(dv_ref)
    lane = lax.broadcasted_iota(jnp.int32, (1, PAIR), 1)
    first = lane < HEAD_DIM
    key_pos = lax.broadcasted_iota(jnp.int32, (1, slots * TILE), 1)
    for t in range(tiles):
        rows = pl.ds(t * TILE, TILE)
        for j in range(slots):
            owner = owner_ref[t, j]
            kbuf[pl.ds(j * TILE, TILE), :] = k_ref[owner]
            vbuf[pl.ds(j * TILE, TILE), :] = v_ref[owner]
        q = q_ref[rows, :]
        g = g_ref[rows, :]
        keys = kbuf[...]
        values = vbuf[...]
        alive = key_pos < length_ref[t] * TILE
        outs = []
        for h in range(2):
            mine = first if h == 0 else jnp.logical_not(first)
            qh = jnp.where(mine, q, jnp.zeros_like(q))
            gh = jnp.where(mine, g, jnp.zeros_like(g))
            scores = _nt(qh, keys) * scale
            scores = jnp.where(alive, scores, NEG_FILL)
            row_max = jnp.max(scores, axis=-1, keepdims=True)
            expo = jnp.exp(scores - row_max)
            weights = expo / jnp.sum(expo, axis=-1, keepdims=True)
            weights_low = weights.astype(jnp.bfloat16)
            attended = _nn(weights_low, values)
            dweights = _nt(gh, values)
            row_delta = jnp.sum(weights * dweights, axis=-1, keepdims=True)
            dscores = (weights * (dweights - row_delta)).astype(jnp.bfloat16)
            query_grad = _nn(dscores, keys)
            key_grad = _tn(dscores, q)
            value_grad = _tn(weights_low, g)
            outs.append((attended, query_grad, key_grad, value_grad))
        pick = lambda i: jnp.where(first, outs[0][i], outs[1][i])
        att_ref[rows, :] = pick(0).astype(att_ref.dtype)
        qg_ref[rows, :] = (pick(1) * scale).astype(qg_ref.dtype)
        key_grad = pick(2) * scale
        value_grad = pick(3)
        for j in range(slots):
            owner = owner_ref[t, j]
            dk_ref[owner] = dk_ref[owner] + key_grad[j * TILE:(j + 1) * TILE]
            dv_ref[owner] = dv_ref[owner] + value_grad[j * TILE:(j + 1) * TILE]
    grad_out[0, :, :, :PAIR] = dk_ref[...].astype(grad_out.dtype)
    grad_out[0, :, :, PAIR:] = dv_ref[...].astype(grad_out.dtype)


def attend_local(owner_of, tile_lengths, queries, cotangent, fetched):
    owners, _, both = fetched.shape
    width = both // 2
    rows = queries.shape[0]
    slots = owner_of.shape[1]
    pairs = width // PAIR
    col = lambda hp, own, ln: (0, hp)
    blk = lambda hp, own, ln: (0, 0, hp)
    grid_spec = pltpu.PrefetchScalarGridSpec(
        num_scalar_prefetch=2,
        grid=(pairs,),
        in_specs=[
            pl.BlockSpec((rows, PAIR), col),
            pl.BlockSpec((rows, PAIR), col),
            pl.BlockSpec((owners, TILE, PAIR), blk),
            pl.BlockSpec((owners, TILE, PAIR), lambda hp, own, ln: (0, 0, hp + pairs)),
        ],
        out_specs=[
            pl.BlockSpec((rows, PAIR), col),
            pl.BlockSpec((rows, PAIR), col),
            pl.BlockSpec((1, owners, TILE, 2 * PAIR), lambda hp, own, ln: (hp, 0, 0, 0)),
        ],
        scratch_shapes=[
            pltpu.VMEM((slots * TILE, PAIR), jnp.bfloat16),
            pltpu.VMEM((slots * TILE, PAIR), jnp.bfloat16),
            pltpu.VMEM((owners, TILE, PAIR), jnp.float32),
            pltpu.VMEM((owners, TILE, PAIR), jnp.float32),
        ],
    )
    return pl.pallas_call(
        attention_kernel,
        grid_spec=grid_spec,
        out_shape=[
            jax.ShapeDtypeStruct((rows, width), jnp.bfloat16),
            jax.ShapeDtypeStruct((rows, width), jnp.bfloat16),
            jax.ShapeDtypeStruct((pairs, owners, TILE, 2 * PAIR), jnp.bfloat16),
        ],
        compiler_params=pltpu.CompilerParams(dimension_semantics=("arbitrary",)),
    )(owner_of, tile_lengths, queries, cotangent, fetched, fetched)


def reply_kernel(pick_ref, k_ref, v_ref, out_ref):
    width = k_ref.shape[2]
    out_ref[0, :, :width] = k_ref[0]
    out_ref[0, :, width:] = v_ref[0]


def gather_reply(picks, key_blocks, value_blocks):
    _, rows, width = key_blocks.shape
    count = picks.shape[0]
    src = lambda i, pick: (pick[i], 0, 0)
    grid_spec = pltpu.PrefetchScalarGridSpec(
        num_scalar_prefetch=1,
        grid=(count,),
        in_specs=[pl.BlockSpec((1, rows, width), src), pl.BlockSpec((1, rows, width), src)],
        out_specs=pl.BlockSpec((1, rows, 2 * width), lambda i, pick: (i, 0, 0)),
    )
    return pl.pallas_call(
        reply_kernel,
        grid_spec=grid_spec,
        out_shape=jax.ShapeDtypeStruct((count, rows, 2 * width), key_blocks.dtype),
    )(picks, key_blocks, value_blocks)


def body(queries, key_rows, value_rows, cotangent, block_lists, tile_lengths):
    owners = lax.axis_size("dim")
    tile_count = block_lists.shape[0]
    slot_count = block_lists.shape[1]
    blocks_here = key_rows.shape[0] // TILE
    model_width = key_rows.shape[1]
    alive_slots = jnp.arange(slot_count, dtype=jnp.int32)[None, :] < tile_lengths[:, None]
    owner_of = block_lists // blocks_here
    local_of = block_lists % blocks_here
    owner_ids = jnp.arange(owners, dtype=jnp.int32)
    matched = (owner_of[:, :, None] == owner_ids[None, None, :]) & alive_slots[:, :, None]
    wanted = jnp.max(jnp.where(matched, local_of[:, :, None], -1), axis=(0, 1))
    requests = lax.all_to_all(
        wanted.reshape(owners, 1), "dim", split_axis=0, concat_axis=0, tiled=True
    )
    block_ids = jnp.arange(blocks_here, dtype=jnp.int32)[None, :]
    picks = jnp.clip(requests.reshape(owners), 0, blocks_here - 1)
    reply = gather_reply(
        picks,
        key_rows.reshape(blocks_here, TILE, model_width),
        value_rows.reshape(blocks_here, TILE, model_width),
    )
    fetched = lax.all_to_all(reply, "dim", split_axis=0, concat_axis=0, tiled=True)
    attended_out, query_grad_out, partial_grads = attend_local(
        owner_of, tile_lengths, queries, cotangent, fetched
    )
    fact_count = lax.axis_size("fact")
    span = model_width // fact_count
    pieces = lax.all_to_all(
        partial_grads.reshape(fact_count * owners, TILE, 2 * span),
        ("fact", "dim"), split_axis=0, concat_axis=0, tiled=True,
    )
    all_requests = lax.all_gather(requests.reshape(owners), "fact", tiled=True)
    block_selector = (all_requests[:, None] == block_ids).astype(jnp.bfloat16)
    summed = jnp.einsum(
        "ep,ejs->pjs", block_selector, pieces, preferred_element_type=jnp.float32
    )
    key_grad_out = summed[:, :, :span].reshape(blocks_here * TILE, span)
    value_grad_out = summed[:, :, span:].reshape(blocks_here * TILE, span)
    return (
        attended_out,
        query_grad_out,
        key_grad_out.astype(jnp.bfloat16),
        value_grad_out.astype(jnp.bfloat16),
    )


def solution(mesh):
    in_specs = (
        P(("fact", "dim"), None),
        P("dim", None),
        P("dim", None),
        P(("fact", "dim"), None),
        P(("fact", "dim"), None),
        P(("fact", "dim")),
    )
    out_specs = (
        P(("fact", "dim"), None),
        P(("fact", "dim"), None),
        P("dim", "fact"),
        P("dim", "fact"),
    )
    return jax.shard_map(body, mesh=mesh, in_specs=in_specs, out_specs=out_specs, check_vma=False)
```

```python
import functools
import jax
import jax.numpy as jnp
from jax import lax
from jax.experimental import pallas as pl
from jax.experimental.pallas import tpu as pltpu
from jax.sharding import PartitionSpec as P

HEADS = 16
HEAD_DIM = 64
TILE = 128
NEG_FILL = -1e30
PAIR = 2 * HEAD_DIM


def _nt(a, b):
    return lax.dot_general(a, b, (((1,), (1,)), ((), ())), preferred_element_type=jnp.float32)


def _tn(a, b):
    return lax.dot_general(a, b, (((0,), (0,)), ((), ())), preferred_element_type=jnp.float32)


def _nn(a, b):
    return jnp.dot(a, b, preferred_element_type=jnp.float32)


def attention_kernel(owner_ref, length_ref, q_ref, g_ref, k_ref, v_ref,
                     att_ref, qg_ref, grad_out, kbuf, vbuf, dk_ref, dv_ref):
    tiles = q_ref.shape[0] // TILE
    slots = kbuf.shape[0] // TILE
    scale = HEAD_DIM ** (-0.5)
    dk_ref[...] = jnp.zeros_like(dk_ref)
    dv_ref[...] = jnp.zeros_like(dv_ref)
    lane = lax.broadcasted_iota(jnp.int32, (1, PAIR), 1)
    first = lane < HEAD_DIM
    key_pos = lax.broadcasted_iota(jnp.int32, (1, slots * TILE), 1)
    for t in range(tiles):
        rows = pl.ds(t * TILE, TILE)
        for j in range(slots):
            owner = owner_ref[t, j]
            kbuf[pl.ds(j * TILE, TILE), :] = k_ref[owner]
            vbuf[pl.ds(j * TILE, TILE), :] = v_ref[owner]
        q = q_ref[rows, :]
        g = g_ref[rows, :]
        keys = kbuf[...]
        values = vbuf[...]
        alive = key_pos < length_ref[t] * TILE
        outs = []
        for h in range(2):
            mine = first if h == 0 else jnp.logical_not(first)
            qh = jnp.where(mine, q, jnp.zeros_like(q))
            gh = jnp.where(mine, g, jnp.zeros_like(g))
            scores = _nt(qh, keys) * scale
            scores = jnp.where(alive, scores, NEG_FILL)
            row_max = jnp.max(scores, axis=-1, keepdims=True)
            expo = jnp.exp(scores - row_max)
            weights = expo / jnp.sum(expo, axis=-1, keepdims=True)
            weights_low = weights.astype(jnp.bfloat16)
            attended = _nn(weights_low, values)
            dweights = _nt(gh, values)
            row_delta = jnp.sum(weights * dweights, axis=-1, keepdims=True)
            dscores = (weights * (dweights - row_delta)).astype(jnp.bfloat16)
            query_grad = _nn(dscores, keys)
            key_grad = _tn(dscores, q)
            value_grad = _tn(weights_low, g)
            outs.append((attended, query_grad, key_grad, value_grad))
        pick = lambda i: jnp.where(first, outs[0][i], outs[1][i])
        att_ref[rows, :] = pick(0).astype(att_ref.dtype)
        qg_ref[rows, :] = (pick(1) * scale).astype(qg_ref.dtype)
        key_grad = pick(2) * scale
        value_grad = pick(3)
        for j in range(slots):
            owner = owner_ref[t, j]
            dk_ref[owner] = dk_ref[owner] + key_grad[j * TILE:(j + 1) * TILE]
            dv_ref[owner] = dv_ref[owner] + value_grad[j * TILE:(j + 1) * TILE]
    grad_out[0, :, :, :PAIR] = dk_ref[...].astype(grad_out.dtype)
    grad_out[0, :, :, PAIR:] = dv_ref[...].astype(grad_out.dtype)


def attend_local(owner_of, tile_lengths, queries, cotangent, fetched):
    owners, _, _, width = fetched.shape
    rows = queries.shape[0]
    slots = owner_of.shape[1]
    pairs = width // PAIR
    col = lambda hp, own, ln: (0, hp)
    blk = lambda hp, own, ln: (0, 0, hp)
    grid_spec = pltpu.PrefetchScalarGridSpec(
        num_scalar_prefetch=2,
        grid=(pairs,),
        in_specs=[
            pl.BlockSpec((rows, PAIR), col),
            pl.BlockSpec((rows, PAIR), col),
            pl.BlockSpec((owners, None, TILE, PAIR), lambda hp, own, ln: (0, 0, 0, hp)),
            pl.BlockSpec((owners, None, TILE, PAIR), lambda hp, own, ln: (0, 1, 0, hp)),
        ],
        out_specs=[
            pl.BlockSpec((rows, PAIR), col),
            pl.BlockSpec((rows, PAIR), col),
            pl.BlockSpec((1, owners, TILE, 2 * PAIR), lambda hp, own, ln: (hp, 0, 0, 0)),
        ],
        scratch_shapes=[
            pltpu.VMEM((slots * TILE, PAIR), jnp.bfloat16),
            pltpu.VMEM((slots * TILE, PAIR), jnp.bfloat16),
            pltpu.VMEM((owners, TILE, PAIR), jnp.float32),
            pltpu.VMEM((owners, TILE, PAIR), jnp.float32),
        ],
    )
    return pl.pallas_call(
        attention_kernel,
        grid_spec=grid_spec,
        out_shape=[
            jax.ShapeDtypeStruct((rows, width), jnp.bfloat16),
            jax.ShapeDtypeStruct((rows, width), jnp.bfloat16),
            jax.ShapeDtypeStruct((pairs, owners, TILE, 2 * PAIR), jnp.bfloat16),
        ],
        compiler_params=pltpu.CompilerParams(dimension_semantics=("arbitrary",)),
    )(owner_of, tile_lengths, queries, cotangent, fetched, fetched)


def reply_kernel(pick_ref, k_hbm, v_hbm, out_hbm, sems):
    copies = []
    for i in range(out_hbm.shape[0]):
        for plane, src in enumerate((k_hbm, v_hbm)):
            copy = pltpu.make_async_copy(src.at[pick_ref[i]], out_hbm.at[i, plane], sems.at[i, plane])
            copy.start()
            copies.append(copy)
    for copy in copies:
        copy.wait()


def gather_reply(picks, key_blocks, value_blocks):
    _, rows, width = key_blocks.shape
    count = picks.shape[0]
    grid_spec = pltpu.PrefetchScalarGridSpec(
        num_scalar_prefetch=1,
        grid=(1,),
        in_specs=[pl.BlockSpec(memory_space=pl.ANY), pl.BlockSpec(memory_space=pl.ANY)],
        out_specs=pl.BlockSpec(memory_space=pl.ANY),
        scratch_shapes=[pltpu.SemaphoreType.DMA((count, 2))],
    )
    return pl.pallas_call(
        reply_kernel,
        grid_spec=grid_spec,
        out_shape=jax.ShapeDtypeStruct((count, 2, rows, width), key_blocks.dtype),
    )(picks, key_blocks, value_blocks)


def sum_kernel(req_ref, piece_ref, key_out, value_out, acc):
    step = pl.program_id(0)
    chunk = piece_ref.shape[0]
    span = key_out.shape[1]
    rows = piece_ref.shape[1]

    @pl.when(step == 0)
    def _():
        acc[...] = jnp.zeros_like(acc)

    for i in range(chunk):
        target = req_ref[step * chunk + i]

        @pl.when(target >= 0)
        def _():
            acc[target] = acc[target] + piece_ref[i].astype(jnp.float32)

    @pl.when(step == pl.num_programs(0) - 1)
    def _():
        for l in range(acc.shape[0]):
            key_out[pl.ds(l * rows, rows), :] = acc[l, :, :span].astype(key_out.dtype)
            value_out[pl.ds(l * rows, rows), :] = acc[l, :, span:].astype(value_out.dtype)


def sum_pieces(all_requests, pieces, blocks):
    sources, rows, both = pieces.shape
    span = both // 2
    chunk = 16
    grid_spec = pltpu.PrefetchScalarGridSpec(
        num_scalar_prefetch=1,
        grid=(sources // chunk,),
        in_specs=[pl.BlockSpec((chunk, rows, both), lambda i, req: (i, 0, 0))],
        out_specs=[
            pl.BlockSpec((blocks * rows, span), lambda i, req: (0, 0)),
            pl.BlockSpec((blocks * rows, span), lambda i, req: (0, 0)),
        ],
        scratch_shapes=[pltpu.VMEM((blocks, rows, both), jnp.float32)],
    )
    return pl.pallas_call(
        sum_kernel,
        grid_spec=grid_spec,
        out_shape=[
            jax.ShapeDtypeStruct((blocks * rows, span), jnp.bfloat16),
            jax.ShapeDtypeStruct((blocks * rows, span), jnp.bfloat16),
        ],
        compiler_params=pltpu.CompilerParams(dimension_semantics=("arbitrary",)),
    )(all_requests, pieces)


def body(queries, key_rows, value_rows, cotangent, block_lists, tile_lengths):
    owners = lax.axis_size("dim")
    tile_count = block_lists.shape[0]
    slot_count = block_lists.shape[1]
    blocks_here = key_rows.shape[0] // TILE
    model_width = key_rows.shape[1]
    alive_slots = jnp.arange(slot_count, dtype=jnp.int32)[None, :] < tile_lengths[:, None]
    owner_of = block_lists // blocks_here
    local_of = block_lists % blocks_here
    owner_ids = jnp.arange(owners, dtype=jnp.int32)
    matched = (owner_of[:, :, None] == owner_ids[None, None, :]) & alive_slots[:, :, None]
    wanted = jnp.max(jnp.where(matched, local_of[:, :, None], -1), axis=(0, 1))
    requests = lax.all_to_all(
        wanted.reshape(owners, 1), "dim", split_axis=0, concat_axis=0, tiled=True
    )
    block_ids = jnp.arange(blocks_here, dtype=jnp.int32)[None, :]
    picks = jnp.clip(requests.reshape(owners), 0, blocks_here - 1)
    reply = gather_reply(
        picks,
        key_rows.reshape(blocks_here, TILE, model_width),
        value_rows.reshape(blocks_here, TILE, model_width),
    )
    fetched = lax.all_to_all(reply, "dim", split_axis=0, concat_axis=0, tiled=True)
    attended_out, query_grad_out, partial_grads = attend_local(
        owner_of, tile_lengths, queries, cotangent, fetched
    )
    fact_count = lax.axis_size("fact")
    span = model_width // fact_count
    pieces = lax.all_to_all(
        partial_grads.reshape(fact_count * owners, TILE, 2 * span),
        ("fact", "dim"), split_axis=0, concat_axis=0, tiled=True,
    )
    all_requests = lax.all_gather(requests.reshape(owners), "fact", tiled=True)
    key_grad_out, value_grad_out = sum_pieces(all_requests, pieces, blocks_here)
    return (
        attended_out,
        query_grad_out,
        key_grad_out,
        value_grad_out,
    )


def solution(mesh):
    in_specs = (
        P(("fact", "dim"), None),
        P("dim", None),
        P("dim", None),
        P(("fact", "dim"), None),
        P(("fact", "dim"), None),
        P(("fact", "dim")),
    )
    out_specs = (
        P(("fact", "dim"), None),
        P(("fact", "dim"), None),
        P("dim", "fact"),
        P("dim", "fact"),
    )
    return jax.shard_map(body, mesh=mesh, in_specs=in_specs, out_specs=out_specs, check_vma=False)
```

```python
import functools
import jax
import jax.numpy as jnp
from jax import lax
from jax.experimental import pallas as pl
from jax.experimental.pallas import tpu as pltpu
from jax.sharding import PartitionSpec as P

HEADS = 16
HEAD_DIM = 64
TILE = 128
NEG_FILL = -1e30
PAIR = 2 * HEAD_DIM


def _nt(a, b):
    return lax.dot_general(a, b, (((1,), (1,)), ((), ())), preferred_element_type=jnp.float32)


def _tn(a, b):
    return lax.dot_general(a, b, (((0,), (0,)), ((), ())), preferred_element_type=jnp.float32)


def _nn(a, b):
    return jnp.dot(a, b, preferred_element_type=jnp.float32)


def pair_attention(q, g, keys, values, alive, first):
    scale = HEAD_DIM ** (-0.5)
    outs = []
    for h in range(2):
        mine = first if h == 0 else jnp.logical_not(first)
        qh = jnp.where(mine, q, jnp.zeros_like(q))
        gh = jnp.where(mine, g, jnp.zeros_like(g))
        scores = _nt(qh, keys) * scale
        scores = jnp.where(alive, scores, NEG_FILL)
        row_max = jnp.max(scores, axis=-1, keepdims=True)
        expo = jnp.exp(scores - row_max)
        weights = expo / jnp.sum(expo, axis=-1, keepdims=True)
        weights_low = weights.astype(jnp.bfloat16)
        attended = _nn(weights_low, values)
        dweights = _nt(gh, values)
        row_delta = jnp.sum(weights * dweights, axis=-1, keepdims=True)
        dscores = (weights * (dweights - row_delta)).astype(jnp.bfloat16)
        query_grad = _nn(dscores, keys)
        key_grad = _tn(dscores, q)
        value_grad = _tn(weights_low, g)
        outs.append((attended, query_grad, key_grad, value_grad))
    pick = lambda i: jnp.where(first, outs[0][i], outs[1][i])
    return pick(0), pick(1) * scale, pick(2) * scale, pick(3)


def fetch_attend_kernel(pick_ref, owner_ref, length_ref, slot_ref, k_ref, v_ref, q_ref, g_ref,
                        att_ref, qg_ref, grad_ref,
                        stage, kbuf, vbuf, gbuf, send_sem, recv_sem, *recv):
    owners = stage.shape[1]
    pairs = stage.shape[0]
    tiles = q_ref.shape[0] // TILE
    slots = kbuf.shape[0] // TILE
    me = lax.axis_index("dim")
    fact = lax.axis_index("fact")
    mesh = pl.DeviceIdType.MESH
    for hp in range(pairs):
        cols = pl.ds(hp * PAIR, PAIR)
        for peer in range(owners):
            chosen = pick_ref[peer]
            stage[hp, peer, 0] = k_ref[chosen, :, cols]
            stage[hp, peer, 1] = v_ref[chosen, :, cols]
    for hp in range(pairs):
        recv[hp][me] = stage[hp, me]
    barrier = pltpu.get_barrier_semaphore()
    for k in range(1, owners):
        pl.semaphore_signal(barrier, inc=1, device_id=(fact, lax.rem(me + k, owners)), device_id_type=mesh)
    pl.semaphore_wait(barrier, owners - 1)

    def remote(hp, k, src):
        dest = lax.rem(me + k, owners)
        return pltpu.make_async_remote_copy(
            src_ref=stage.at[hp, dest],
            dst_ref=recv[hp].at[src],
            send_sem=send_sem.at[hp, dest],
            recv_sem=recv_sem.at[hp, src],
            device_id=(fact, dest),
            device_id_type=mesh,
        )

    for hp in range(pairs):
        for k in range(1, owners):
            remote(hp, k, me).start()

    gbuf[:, slots] = jnp.zeros(gbuf.shape[:1] + gbuf.shape[2:], gbuf.dtype)
    lane = lax.broadcasted_iota(jnp.int32, (1, PAIR), 1)
    first = lane < HEAD_DIM
    key_pos = lax.broadcasted_iota(jnp.int32, (1, slots * TILE), 1)
    for hp in range(pairs):
        cols = pl.ds(hp * PAIR, PAIR)
        for k in range(1, owners):
            remote(hp, owners - k, lax.rem(me + k, owners)).wait_recv()
        for t in range(tiles):
            rows = pl.ds(t * TILE, TILE)
            for j in range(slots):
                owner = owner_ref[t, j]
                kbuf[pl.ds(j * TILE, TILE), :] = recv[hp][owner, 0]
                vbuf[pl.ds(j * TILE, TILE), :] = recv[hp][owner, 1]
            alive = key_pos < length_ref[t] * TILE
            attended, query_grad, key_grad, value_grad = pair_attention(
                q_ref[rows, cols], g_ref[rows, cols], kbuf[...], vbuf[...], alive, first
            )
            att_ref[rows, cols] = attended.astype(att_ref.dtype)
            qg_ref[rows, cols] = query_grad.astype(qg_ref.dtype)
            for j in range(slots):
                gbuf[t, j, :, :PAIR] = key_grad[j * TILE:(j + 1) * TILE]
                gbuf[t, j, :, PAIR:] = value_grad[j * TILE:(j + 1) * TILE]
        for owner in range(owners):
            total = gbuf[0, slot_ref[0, owner]]
            for t in range(1, tiles):
                total = total + gbuf[t, slot_ref[t, owner]]
            grad_ref[hp, owner] = total.astype(grad_ref.dtype)
    for hp in range(pairs):
        for k in range(1, owners):
            remote(hp, k, me).wait_send()


def fetch_attend(picks, owner_of, tile_lengths, slot_of, key_blocks, value_blocks, queries, cotangent):
    _, _, width = key_blocks.shape
    owners = picks.shape[0]
    rows = queries.shape[0]
    slots = owner_of.shape[1]
    pairs = width // PAIR
    whole = pl.BlockSpec(memory_space=pltpu.VMEM)
    grid_spec = pltpu.PrefetchScalarGridSpec(
        num_scalar_prefetch=4,
        grid=(1,),
        in_specs=[whole] * 4,
        out_specs=[whole] * 3,
        scratch_shapes=[
            pltpu.VMEM((pairs, owners, 2, TILE, PAIR), jnp.bfloat16),
            pltpu.VMEM((slots * TILE, PAIR), jnp.bfloat16),
            pltpu.VMEM((slots * TILE, PAIR), jnp.bfloat16),
            pltpu.VMEM((rows // TILE, slots + 1, TILE, 2 * PAIR), jnp.float32),
            pltpu.SemaphoreType.DMA((pairs, owners)),
            pltpu.SemaphoreType.DMA((pairs, owners)),
        ] + [pltpu.VMEM((owners, 2, TILE, PAIR), jnp.bfloat16) for _ in range(pairs)],
    )
    return pl.pallas_call(
        fetch_attend_kernel,
        grid_spec=grid_spec,
        out_shape=[
            jax.ShapeDtypeStruct((rows, width), jnp.bfloat16),
            jax.ShapeDtypeStruct((rows, width), jnp.bfloat16),
            jax.ShapeDtypeStruct((pairs, owners, TILE, 2 * PAIR), jnp.bfloat16),
        ],
        compiler_params=pltpu.CompilerParams(
            collective_id=0, has_side_effects=True, vmem_limit_bytes=60 * 1024 * 1024
        ),
    )(picks, owner_of, tile_lengths, slot_of, key_blocks, value_blocks, queries, cotangent)


def sum_kernel(req_ref, piece_ref, key_out, value_out, acc):
    step = pl.program_id(0)
    chunk = piece_ref.shape[0]
    span = key_out.shape[1]
    rows = piece_ref.shape[1]

    @pl.when(step == 0)
    def _():
        acc[...] = jnp.zeros_like(acc)

    for i in range(chunk):
        target = req_ref[step * chunk + i]

        @pl.when(target >= 0)
        def _():
            acc[target] = acc[target] + piece_ref[i].astype(jnp.float32)

    @pl.when(step == pl.num_programs(0) - 1)
    def _():
        for l in range(acc.shape[0]):
            key_out[pl.ds(l * rows, rows), :] = acc[l, :, :span].astype(key_out.dtype)
            value_out[pl.ds(l * rows, rows), :] = acc[l, :, span:].astype(value_out.dtype)


def sum_pieces(all_requests, pieces, blocks):
    sources, rows, both = pieces.shape
    span = both // 2
    chunk = 16
    grid_spec = pltpu.PrefetchScalarGridSpec(
        num_scalar_prefetch=1,
        grid=(sources // chunk,),
        in_specs=[pl.BlockSpec((chunk, rows, both), lambda i, req: (i, 0, 0))],
        out_specs=[
            pl.BlockSpec((blocks * rows, span), lambda i, req: (0, 0)),
            pl.BlockSpec((blocks * rows, span), lambda i, req: (0, 0)),
        ],
        scratch_shapes=[pltpu.VMEM((blocks, rows, both), jnp.float32)],
    )
    return pl.pallas_call(
        sum_kernel,
        grid_spec=grid_spec,
        out_shape=[
            jax.ShapeDtypeStruct((blocks * rows, span), jnp.bfloat16),
            jax.ShapeDtypeStruct((blocks * rows, span), jnp.bfloat16),
        ],
        compiler_params=pltpu.CompilerParams(dimension_semantics=("arbitrary",)),
    )(all_requests, pieces)


def body(queries, key_rows, value_rows, cotangent, block_lists, tile_lengths):
    owners = lax.axis_size("dim")
    tile_count = block_lists.shape[0]
    slot_count = block_lists.shape[1]
    blocks_here = key_rows.shape[0] // TILE
    model_width = key_rows.shape[1]
    alive_slots = jnp.arange(slot_count, dtype=jnp.int32)[None, :] < tile_lengths[:, None]
    owner_of = jnp.clip(block_lists // blocks_here, 0, owners - 1)
    local_of = block_lists % blocks_here
    owner_ids = jnp.arange(owners, dtype=jnp.int32)
    matched = (owner_of[:, :, None] == owner_ids[None, None, :]) & alive_slots[:, :, None]
    wanted = jnp.max(jnp.where(matched, local_of[:, :, None], -1), axis=(0, 1))
    requests = lax.all_to_all(
        wanted.reshape(owners, 1), "dim", split_axis=0, concat_axis=0, tiled=True
    )
    block_ids = jnp.arange(blocks_here, dtype=jnp.int32)[None, :]
    picks = jnp.clip(requests.reshape(owners), 0, blocks_here - 1)
    slot_ids = jnp.arange(slot_count, dtype=jnp.int32)[None, :, None]
    live_match = (owner_of[:, :, None] == owner_ids[None, None, :]) & alive_slots[:, :, None]
    slot_of = jnp.min(jnp.where(live_match, slot_ids, slot_count), axis=1)
    attended_out, query_grad_out, partial_grads = fetch_attend(
        picks,
        owner_of,
        tile_lengths,
        slot_of,
        key_rows.reshape(blocks_here, TILE, model_width),
        value_rows.reshape(blocks_here, TILE, model_width),
        queries,
        cotangent,
    )
    fact_count = lax.axis_size("fact")
    span = model_width // fact_count
    pieces = lax.all_to_all(
        partial_grads.reshape(fact_count * owners, TILE, 2 * span),
        ("fact", "dim"), split_axis=0, concat_axis=0, tiled=True,
    )
    all_requests = lax.all_gather(requests.reshape(owners), "fact", tiled=True)
    key_grad_out, value_grad_out = sum_pieces(all_requests, pieces, blocks_here)
    return (
        attended_out,
        query_grad_out,
        key_grad_out,
        value_grad_out,
    )


def solution(mesh):
    in_specs = (
        P(("fact", "dim"), None),
        P("dim", None),
        P("dim", None),
        P(("fact", "dim"), None),
        P(("fact", "dim"), None),
        P(("fact", "dim")),
    )
    out_specs = (
        P(("fact", "dim"), None),
        P(("fact", "dim"), None),
        P("dim", "fact"),
        P("dim", "fact"),
    )
    return jax.shard_map(body, mesh=mesh, in_specs=in_specs, out_specs=out_specs, check_vma=False)
```

```python
import functools
import jax
import jax.numpy as jnp
from jax import lax
from jax.experimental import pallas as pl
from jax.experimental.pallas import tpu as pltpu
from jax.sharding import PartitionSpec as P

HEADS = 16
HEAD_DIM = 64
TILE = 128
NEG_FILL = -1e30
PAIR = 2 * HEAD_DIM


def _nt(a, b):
    return lax.dot_general(a, b, (((1,), (1,)), ((), ())), preferred_element_type=jnp.float32)


def _tn(a, b):
    return lax.dot_general(a, b, (((0,), (0,)), ((), ())), preferred_element_type=jnp.float32)


def _nn(a, b):
    return jnp.dot(a, b, preferred_element_type=jnp.float32)


def pair_attention(q, g, keys, values, alive, first):
    scale = HEAD_DIM ** (-0.5)
    outs = []
    for h in range(2):
        mine = first if h == 0 else jnp.logical_not(first)
        qh = jnp.where(mine, q, jnp.zeros_like(q))
        gh = jnp.where(mine, g, jnp.zeros_like(g))
        scores = _nt(qh, keys) * scale
        scores = jnp.where(alive, scores, NEG_FILL)
        row_max = jnp.max(scores, axis=-1, keepdims=True)
        expo = jnp.exp(scores - row_max)
        weights = expo / jnp.sum(expo, axis=-1, keepdims=True)
        weights_low = weights.astype(jnp.bfloat16)
        attended = _nn(weights_low, values)
        dweights = _nt(gh, values)
        row_delta = jnp.sum(weights * dweights, axis=-1, keepdims=True)
        dscores = (weights * (dweights - row_delta)).astype(jnp.bfloat16)
        query_grad = _nn(dscores, keys)
        key_grad = _tn(dscores, q)
        value_grad = _tn(weights_low, g)
        outs.append((attended, query_grad, key_grad, value_grad))
    pick = lambda i: jnp.where(first, outs[0][i], outs[1][i])
    return pick(0), pick(1) * scale, pick(2) * scale, pick(3)


def fetch_attend_kernel(pick_ref, owner_ref, length_ref, slot_ref, k_ref, v_ref, q_ref, g_ref,
                        att_ref, qg_ref, grad_ref,
                        stage, kbuf, vbuf, gbuf, gsend, send_sem, recv_sem, gsend_sem, grecv_sem,
                        *recv):
    owners = stage.shape[1]
    pairs = stage.shape[0]
    tiles = q_ref.shape[0] // TILE
    slots = kbuf.shape[0] // TILE
    me = lax.axis_index("dim")
    fact = lax.axis_index("fact")
    mesh = pl.DeviceIdType.MESH
    for hp in range(pairs):
        cols = pl.ds(hp * PAIR, PAIR)
        for peer in range(owners):
            chosen = pick_ref[peer]
            stage[hp, peer, 0] = k_ref[chosen, :, cols]
            stage[hp, peer, 1] = v_ref[chosen, :, cols]
    for hp in range(pairs):
        recv[hp][me] = stage[hp, me]
    facts = pairs
    others = [(fo, k) for fo in range(facts) for k in range(owners) if (fo, k) != (0, 0)]
    barrier = pltpu.get_barrier_semaphore()
    for fo, k in others:
        pl.semaphore_signal(
            barrier, inc=1,
            device_id=(lax.rem(fact + fo, facts), lax.rem(me + k, owners)), device_id_type=mesh,
        )
    pl.semaphore_wait(barrier, len(others))
    own_slot = fact * owners + me

    def grad_remote(hp, dest, slot):
        return pltpu.make_async_remote_copy(
            src_ref=gsend.at[hp, dest],
            dst_ref=grad_ref.at[slot],
            send_sem=gsend_sem.at[hp, dest],
            recv_sem=grecv_sem.at[slot],
            device_id=(hp, dest),
            device_id_type=mesh,
        )

    def grad_local(hp):
        return pltpu.make_async_copy(gsend.at[hp, me], grad_ref.at[own_slot], grecv_sem.at[own_slot])

    def remote(hp, k, src):
        dest = lax.rem(me + k, owners)
        return pltpu.make_async_remote_copy(
            src_ref=stage.at[hp, dest],
            dst_ref=recv[hp].at[src],
            send_sem=send_sem.at[hp, dest],
            recv_sem=recv_sem.at[hp, src],
            device_id=(fact, dest),
            device_id_type=mesh,
        )

    for hp in range(pairs):
        for k in range(1, owners):
            remote(hp, k, me).start()

    gbuf[:, slots] = jnp.zeros(gbuf.shape[:1] + gbuf.shape[2:], gbuf.dtype)
    lane = lax.broadcasted_iota(jnp.int32, (1, PAIR), 1)
    first = lane < HEAD_DIM
    key_pos = lax.broadcasted_iota(jnp.int32, (1, slots * TILE), 1)
    for hp in range(pairs):
        cols = pl.ds(hp * PAIR, PAIR)
        for k in range(1, owners):
            remote(hp, owners - k, lax.rem(me + k, owners)).wait_recv()
        for t in range(tiles):
            rows = pl.ds(t * TILE, TILE)
            for j in range(slots):
                owner = owner_ref[t, j]
                kbuf[pl.ds(j * TILE, TILE), :] = recv[hp][owner, 0]
                vbuf[pl.ds(j * TILE, TILE), :] = recv[hp][owner, 1]
            alive = key_pos < length_ref[t] * TILE
            attended, query_grad, key_grad, value_grad = pair_attention(
                q_ref[rows, cols], g_ref[rows, cols], kbuf[...], vbuf[...], alive, first
            )
            att_ref[rows, cols] = attended.astype(att_ref.dtype)
            qg_ref[rows, cols] = query_grad.astype(qg_ref.dtype)
            for j in range(slots):
                gbuf[t, j, :, :PAIR] = key_grad[j * TILE:(j + 1) * TILE]
                gbuf[t, j, :, PAIR:] = value_grad[j * TILE:(j + 1) * TILE]
        for owner in range(owners):
            total = gbuf[0, slot_ref[0, owner]]
            for t in range(1, tiles):
                total = total + gbuf[t, slot_ref[t, owner]]
            gsend[hp, owner] = total.astype(gsend.dtype)
        for k in range(1, owners):
            grad_remote(hp, lax.rem(me + k, owners), own_slot).start()

        @pl.when(fact != hp)
        def _():
            grad_remote(hp, me, own_slot).start()

        @pl.when(fact == hp)
        def _():
            grad_local(hp).start()

    for hp in range(pairs):
        for k in range(1, owners):
            remote(hp, k, me).wait_send()
    for fo, k in others:
        slot = lax.rem(fact + fo, facts) * owners + lax.rem(me + k, owners)
        grad_remote(0, me, slot).wait_recv()
    for hp in range(pairs):
        for k in range(1, owners):
            grad_remote(hp, lax.rem(me + k, owners), own_slot).wait_send()

        @pl.when(fact != hp)
        def _():
            grad_remote(hp, me, own_slot).wait_send()

        @pl.when(fact == hp)
        def _():
            grad_local(hp).wait()


def fetch_attend(picks, owner_of, tile_lengths, slot_of, key_blocks, value_blocks, queries, cotangent):
    _, _, width = key_blocks.shape
    owners = picks.shape[0]
    rows = queries.shape[0]
    slots = owner_of.shape[1]
    pairs = width // PAIR
    whole = pl.BlockSpec(memory_space=pltpu.VMEM)
    grid_spec = pltpu.PrefetchScalarGridSpec(
        num_scalar_prefetch=4,
        grid=(1,),
        in_specs=[whole] * 4,
        out_specs=[whole, whole, pl.BlockSpec(memory_space=pl.ANY)],
        scratch_shapes=[
            pltpu.VMEM((pairs, owners, 2, TILE, PAIR), jnp.bfloat16),
            pltpu.VMEM((slots * TILE, PAIR), jnp.bfloat16),
            pltpu.VMEM((slots * TILE, PAIR), jnp.bfloat16),
            pltpu.VMEM((rows // TILE, slots + 1, TILE, 2 * PAIR), jnp.float32),
            pltpu.VMEM((pairs, owners, TILE, 2 * PAIR), jnp.bfloat16),
            pltpu.SemaphoreType.DMA((pairs, owners)),
            pltpu.SemaphoreType.DMA((pairs, owners)),
            pltpu.SemaphoreType.DMA((pairs, owners)),
            pltpu.SemaphoreType.DMA((pairs * owners,)),
        ] + [pltpu.VMEM((owners, 2, TILE, PAIR), jnp.bfloat16) for _ in range(pairs)],
    )
    return pl.pallas_call(
        fetch_attend_kernel,
        grid_spec=grid_spec,
        out_shape=[
            jax.ShapeDtypeStruct((rows, width), jnp.bfloat16),
            jax.ShapeDtypeStruct((rows, width), jnp.bfloat16),
            jax.ShapeDtypeStruct((pairs * owners, TILE, 2 * PAIR), jnp.bfloat16),
        ],
        compiler_params=pltpu.CompilerParams(
            collective_id=0, has_side_effects=True, vmem_limit_bytes=60 * 1024 * 1024
        ),
    )(picks, owner_of, tile_lengths, slot_of, key_blocks, value_blocks, queries, cotangent)


def sum_kernel(req_ref, piece_ref, key_out, value_out, acc):
    step = pl.program_id(0)
    chunk = piece_ref.shape[0]
    span = key_out.shape[1]
    rows = piece_ref.shape[1]

    @pl.when(step == 0)
    def _():
        acc[...] = jnp.zeros_like(acc)

    for i in range(chunk):
        target = req_ref[step * chunk + i]

        @pl.when(target >= 0)
        def _():
            acc[target] = acc[target] + piece_ref[i].astype(jnp.float32)

    @pl.when(step == pl.num_programs(0) - 1)
    def _():
        for l in range(acc.shape[0]):
            key_out[pl.ds(l * rows, rows), :] = acc[l, :, :span].astype(key_out.dtype)
            value_out[pl.ds(l * rows, rows), :] = acc[l, :, span:].astype(value_out.dtype)


def sum_pieces(all_requests, pieces, blocks):
    sources, rows, both = pieces.shape
    span = both // 2
    chunk = 16
    grid_spec = pltpu.PrefetchScalarGridSpec(
        num_scalar_prefetch=1,
        grid=(sources // chunk,),
        in_specs=[pl.BlockSpec((chunk, rows, both), lambda i, req: (i, 0, 0))],
        out_specs=[
            pl.BlockSpec((blocks * rows, span), lambda i, req: (0, 0)),
            pl.BlockSpec((blocks * rows, span), lambda i, req: (0, 0)),
        ],
        scratch_shapes=[pltpu.VMEM((blocks, rows, both), jnp.float32)],
    )
    return pl.pallas_call(
        sum_kernel,
        grid_spec=grid_spec,
        out_shape=[
            jax.ShapeDtypeStruct((blocks * rows, span), jnp.bfloat16),
            jax.ShapeDtypeStruct((blocks * rows, span), jnp.bfloat16),
        ],
        compiler_params=pltpu.CompilerParams(dimension_semantics=("arbitrary",)),
    )(all_requests, pieces)


def body(queries, key_rows, value_rows, cotangent, block_lists, tile_lengths):
    owners = lax.axis_size("dim")
    tile_count = block_lists.shape[0]
    slot_count = block_lists.shape[1]
    blocks_here = key_rows.shape[0] // TILE
    model_width = key_rows.shape[1]
    alive_slots = jnp.arange(slot_count, dtype=jnp.int32)[None, :] < tile_lengths[:, None]
    owner_of = jnp.clip(block_lists // blocks_here, 0, owners - 1)
    local_of = block_lists % blocks_here
    owner_ids = jnp.arange(owners, dtype=jnp.int32)
    matched = (owner_of[:, :, None] == owner_ids[None, None, :]) & alive_slots[:, :, None]
    wanted = jnp.max(jnp.where(matched, local_of[:, :, None], -1), axis=(0, 1))
    requests = lax.all_to_all(
        wanted.reshape(owners, 1), "dim", split_axis=0, concat_axis=0, tiled=True
    )
    block_ids = jnp.arange(blocks_here, dtype=jnp.int32)[None, :]
    picks = jnp.clip(requests.reshape(owners), 0, blocks_here - 1)
    slot_ids = jnp.arange(slot_count, dtype=jnp.int32)[None, :, None]
    live_match = (owner_of[:, :, None] == owner_ids[None, None, :]) & alive_slots[:, :, None]
    slot_of = jnp.min(jnp.where(live_match, slot_ids, slot_count), axis=1)
    attended_out, query_grad_out, partial_grads = fetch_attend(
        picks,
        owner_of,
        tile_lengths,
        slot_of,
        key_rows.reshape(blocks_here, TILE, model_width),
        value_rows.reshape(blocks_here, TILE, model_width),
        queries,
        cotangent,
    )
    pieces = partial_grads
    all_requests = lax.all_gather(requests.reshape(owners), "fact", tiled=True)
    key_grad_out, value_grad_out = sum_pieces(all_requests, pieces, blocks_here)
    return (
        attended_out,
        query_grad_out,
        key_grad_out,
        value_grad_out,
    )


def solution(mesh):
    in_specs = (
        P(("fact", "dim"), None),
        P("dim", None),
        P("dim", None),
        P(("fact", "dim"), None),
        P(("fact", "dim"), None),
        P(("fact", "dim")),
    )
    out_specs = (
        P(("fact", "dim"), None),
        P(("fact", "dim"), None),
        P("dim", "fact"),
        P("dim", "fact"),
    )
    return jax.shard_map(body, mesh=mesh, in_specs=in_specs, out_specs=out_specs, check_vma=False)
```

```python
import functools
import jax
import jax.numpy as jnp
from jax import lax
from jax.experimental import pallas as pl
from jax.experimental.pallas import tpu as pltpu
from jax.sharding import PartitionSpec as P

HEADS = 16
HEAD_DIM = 64
TILE = 128
NEG_FILL = -1e30
PAIR = 2 * HEAD_DIM


def _nt(a, b):
    return lax.dot_general(a, b, (((1,), (1,)), ((), ())), preferred_element_type=jnp.float32)


def _tn(a, b):
    return lax.dot_general(a, b, (((0,), (0,)), ((), ())), preferred_element_type=jnp.float32)


def _nn(a, b):
    return jnp.dot(a, b, preferred_element_type=jnp.float32)


def pair_attention(q, g, keys, values, alive, first):
    scale = HEAD_DIM ** (-0.5)
    outs = []
    for h in range(2):
        mine = first if h == 0 else jnp.logical_not(first)
        qh = jnp.where(mine, q, jnp.zeros_like(q))
        gh = jnp.where(mine, g, jnp.zeros_like(g))
        scores = _nt(qh, keys) * scale
        scores = jnp.where(alive, scores, NEG_FILL)
        row_max = jnp.max(scores, axis=-1, keepdims=True)
        expo = jnp.exp(scores - row_max)
        weights = expo / jnp.sum(expo, axis=-1, keepdims=True)
        weights_low = weights.astype(jnp.bfloat16)
        attended = _nn(weights_low, values)
        dweights = _nt(gh, values)
        row_delta = jnp.sum(weights * dweights, axis=-1, keepdims=True)
        dscores = (weights * (dweights - row_delta)).astype(jnp.bfloat16)
        query_grad = _nn(dscores, keys)
        key_grad = _tn(dscores, q)
        value_grad = _tn(weights_low, g)
        outs.append((attended, query_grad, key_grad, value_grad))
    pick = lambda i: jnp.where(first, outs[0][i], outs[1][i])
    return pick(0), pick(1) * scale, pick(2) * scale, pick(3)


def fetch_attend_kernel(pick_ref, owner_ref, length_ref, slot_ref, k_ref, v_ref, q_ref, g_ref,
                        att_ref, qg_ref, grad_ref,
                        stage, kbuf, vbuf, gbuf, send_sem, recv_sem, *recv):
    owners = stage.shape[1]
    pairs = stage.shape[0]
    tiles = q_ref.shape[0] // TILE
    slots = kbuf.shape[0] // TILE
    me = lax.axis_index("dim")
    fact = lax.axis_index("fact")
    mesh = pl.DeviceIdType.MESH
    for hp in range(pairs):
        cols = pl.ds(hp * PAIR, PAIR)
        for peer in range(owners):
            chosen = pick_ref[peer]
            stage[hp, peer, 0] = k_ref[chosen, :, cols]
            stage[hp, peer, 1] = v_ref[chosen, :, cols]
    for hp in range(pairs):
        recv[hp][me] = stage[hp, me]
    barrier = pltpu.get_barrier_semaphore()
    for k in range(1, owners):
        pl.semaphore_signal(barrier, inc=1, device_id=(fact, lax.rem(me + k, owners)), device_id_type=mesh)
    pl.semaphore_wait(barrier, owners - 1)

    def remote(hp, k, src):
        dest = lax.rem(me + k, owners)
        return pltpu.make_async_remote_copy(
            src_ref=stage.at[hp, dest],
            dst_ref=recv[hp].at[src],
            send_sem=send_sem.at[hp, dest],
            recv_sem=recv_sem.at[hp, src],
            device_id=(fact, dest),
            device_id_type=mesh,
        )

    for hp in range(pairs):
        for k in range(1, owners):
            remote(hp, k, me).start()

    gbuf[:, slots] = jnp.zeros(gbuf.shape[:1] + gbuf.shape[2:], gbuf.dtype)
    lane = lax.broadcasted_iota(jnp.int32, (1, PAIR), 1)
    first = lane < HEAD_DIM
    key_pos = lax.broadcasted_iota(jnp.int32, (1, slots * TILE), 1)
    for hp in range(pairs):
        cols = pl.ds(hp * PAIR, PAIR)
        for k in range(1, owners):
            remote(hp, owners - k, lax.rem(me + k, owners)).wait_recv()
        for t in range(tiles):
            rows = pl.ds(t * TILE, TILE)
            for j in range(slots):
                owner = owner_ref[t, j]
                kbuf[pl.ds(j * TILE, TILE), :] = recv[hp][owner, 0]
                vbuf[pl.ds(j * TILE, TILE), :] = recv[hp][owner, 1]
            alive = key_pos < length_ref[t] * TILE
            attended, query_grad, key_grad, value_grad = pair_attention(
                q_ref[rows, cols], g_ref[rows, cols], kbuf[...], vbuf[...], alive, first
            )
            att_ref[rows, cols] = attended.astype(att_ref.dtype)
            qg_ref[rows, cols] = query_grad.astype(qg_ref.dtype)
            for j in range(slots):
                gbuf[t, j, :, :PAIR] = key_grad[j * TILE:(j + 1) * TILE]
                gbuf[t, j, :, PAIR:] = value_grad[j * TILE:(j + 1) * TILE]
        for owner in range(owners):
            total = gbuf[0, slot_ref[0, owner]]
            for t in range(1, tiles):
                total = total + gbuf[t, slot_ref[t, owner]]
            grad_ref[hp, owner] = total.astype(grad_ref.dtype)
    for hp in range(pairs):
        for k in range(1, owners):
            remote(hp, k, me).wait_send()


def fetch_attend(picks, owner_of, tile_lengths, slot_of, key_blocks, value_blocks, queries, cotangent):
    _, _, width = key_blocks.shape
    owners = picks.shape[0]
    rows = queries.shape[0]
    slots = owner_of.shape[1]
    pairs = width // PAIR
    whole = pl.BlockSpec(memory_space=pltpu.VMEM)
    grid_spec = pltpu.PrefetchScalarGridSpec(
        num_scalar_prefetch=4,
        grid=(1,),
        in_specs=[whole] * 4,
        out_specs=[whole] * 3,
        scratch_shapes=[
            pltpu.VMEM((pairs, owners, 2, TILE, PAIR), jnp.bfloat16),
            pltpu.VMEM((slots * TILE, PAIR), jnp.bfloat16),
            pltpu.VMEM((slots * TILE, PAIR), jnp.bfloat16),
            pltpu.VMEM((rows // TILE, slots + 1, TILE, 2 * PAIR), jnp.float32),
            pltpu.SemaphoreType.DMA((pairs, owners)),
            pltpu.SemaphoreType.DMA((pairs, owners)),
        ] + [pltpu.VMEM((owners, 2, TILE, PAIR), jnp.bfloat16) for _ in range(pairs)],
    )
    return pl.pallas_call(
        fetch_attend_kernel,
        grid_spec=grid_spec,
        out_shape=[
            jax.ShapeDtypeStruct((rows, width), jnp.bfloat16),
            jax.ShapeDtypeStruct((rows, width), jnp.bfloat16),
            jax.ShapeDtypeStruct((pairs, owners, TILE, 2 * PAIR), jnp.bfloat16),
        ],
        compiler_params=pltpu.CompilerParams(
            collective_id=0, has_side_effects=True, vmem_limit_bytes=60 * 1024 * 1024
        ),
    )(picks, owner_of, tile_lengths, slot_of, key_blocks, value_blocks, queries, cotangent)


def sum_kernel(sel_ref, piece_ref, out_ref):
    out_ref[...] = jnp.dot(sel_ref[...], piece_ref[...], preferred_element_type=jnp.float32)


def sum_pieces(all_requests, pieces, blocks):
    sources, rows, both = pieces.shape
    span = both // 2
    flat = pieces.reshape(sources, rows * both)
    chunk = 4096
    block_ids = jnp.arange(blocks, dtype=jnp.int32)[:, None]
    selector = (all_requests[None, :] == block_ids).astype(pieces.dtype)
    summed = pl.pallas_call(
        sum_kernel,
        grid=(rows * both // chunk,),
        in_specs=[
            pl.BlockSpec((blocks, sources), lambda i: (0, 0)),
            pl.BlockSpec((sources, chunk), lambda i: (0, i)),
        ],
        out_specs=pl.BlockSpec((blocks, chunk), lambda i: (0, i)),
        out_shape=jax.ShapeDtypeStruct((blocks, rows * both), jnp.float32),
    )(selector, flat).reshape(blocks, rows, both)
    key_grad = summed[:, :, :span].reshape(blocks * rows, span).astype(jnp.bfloat16)
    value_grad = summed[:, :, span:].reshape(blocks * rows, span).astype(jnp.bfloat16)
    return key_grad, value_grad


def body(queries, key_rows, value_rows, cotangent, block_lists, tile_lengths):
    owners = lax.axis_size("dim")
    tile_count = block_lists.shape[0]
    slot_count = block_lists.shape[1]
    blocks_here = key_rows.shape[0] // TILE
    model_width = key_rows.shape[1]
    alive_slots = jnp.arange(slot_count, dtype=jnp.int32)[None, :] < tile_lengths[:, None]
    owner_of = jnp.clip(block_lists // blocks_here, 0, owners - 1)
    local_of = block_lists % blocks_here
    owner_ids = jnp.arange(owners, dtype=jnp.int32)
    matched = (owner_of[:, :, None] == owner_ids[None, None, :]) & alive_slots[:, :, None]
    wanted = jnp.max(jnp.where(matched, local_of[:, :, None], -1), axis=(0, 1))
    requests = lax.all_to_all(
        wanted.reshape(owners, 1), "dim", split_axis=0, concat_axis=0, tiled=True
    )
    block_ids = jnp.arange(blocks_here, dtype=jnp.int32)[None, :]
    picks = jnp.clip(requests.reshape(owners), 0, blocks_here - 1)
    slot_ids = jnp.arange(slot_count, dtype=jnp.int32)[None, :, None]
    live_match = (owner_of[:, :, None] == owner_ids[None, None, :]) & alive_slots[:, :, None]
    slot_of = jnp.min(jnp.where(live_match, slot_ids, slot_count), axis=1)
    attended_out, query_grad_out, partial_grads = fetch_attend(
        picks,
        owner_of,
        tile_lengths,
        slot_of,
        key_rows.reshape(blocks_here, TILE, model_width),
        value_rows.reshape(blocks_here, TILE, model_width),
        queries,
        cotangent,
    )
    fact_count = lax.axis_size("fact")
    span = model_width // fact_count
    pieces = lax.all_to_all(
        partial_grads.reshape(fact_count * owners, TILE, 2 * span),
        ("fact", "dim"), split_axis=0, concat_axis=0, tiled=True,
    )
    all_requests = lax.all_gather(requests.reshape(owners), "fact", tiled=True)
    key_grad_out, value_grad_out = sum_pieces(all_requests, pieces, blocks_here)
    return (
        attended_out,
        query_grad_out,
        key_grad_out,
        value_grad_out,
    )


def solution(mesh):
    in_specs = (
        P(("fact", "dim"), None),
        P("dim", None),
        P("dim", None),
        P(("fact", "dim"), None),
        P(("fact", "dim"), None),
        P(("fact", "dim")),
    )
    out_specs = (
        P(("fact", "dim"), None),
        P(("fact", "dim"), None),
        P("dim", "fact"),
        P("dim", "fact"),
    )
    return jax.shard_map(body, mesh=mesh, in_specs=in_specs, out_specs=out_specs, check_vma=False)
```

```python
import functools
import jax
import jax.numpy as jnp
from jax import lax
from jax.experimental import pallas as pl
from jax.experimental.pallas import tpu as pltpu
from jax.sharding import PartitionSpec as P

HEADS = 16
HEAD_DIM = 64
TILE = 128
NEG_FILL = -1e30
PAIR = 2 * HEAD_DIM


def _nt(a, b):
    return lax.dot_general(a, b, (((1,), (1,)), ((), ())), preferred_element_type=jnp.float32)


def _tn(a, b):
    return lax.dot_general(a, b, (((0,), (0,)), ((), ())), preferred_element_type=jnp.float32)


def _nn(a, b):
    return jnp.dot(a, b, preferred_element_type=jnp.float32)


def pair_attention(q, g, keys, values, alive, first):
    scale = HEAD_DIM ** (-0.5)
    outs = []
    for h in range(2):
        mine = first if h == 0 else jnp.logical_not(first)
        qh = jnp.where(mine, q, jnp.zeros_like(q))
        gh = jnp.where(mine, g, jnp.zeros_like(g))
        scores = _nt(qh, keys) * scale
        scores = jnp.where(alive, scores, NEG_FILL)
        row_max = jnp.max(scores, axis=-1, keepdims=True)
        expo = jnp.exp(scores - row_max)
        weights = expo / jnp.sum(expo, axis=-1, keepdims=True)
        weights_low = weights.astype(jnp.bfloat16)
        attended = _nn(weights_low, values)
        dweights = _nt(gh, values)
        row_delta = jnp.sum(weights * dweights, axis=-1, keepdims=True)
        dscores = (weights * (dweights - row_delta)).astype(jnp.bfloat16)
        query_grad = _nn(dscores, keys)
        key_grad = _tn(dscores, q)
        value_grad = _tn(weights_low, g)
        outs.append((attended, query_grad, key_grad, value_grad))
    pick = lambda i: jnp.where(first, outs[0][i], outs[1][i])
    return pick(0), pick(1) * scale, pick(2) * scale, pick(3)


def fetch_attend_kernel(pick_ref, owner_ref, length_ref, slot_ref, k_ref, v_ref, q_ref, g_ref,
                        att_ref, qg_ref, grad_ref,
                        stage, kbuf, vbuf, gbuf, send_sem, recv_sem, *recv):
    owners = stage.shape[1]
    pairs = stage.shape[0]
    tiles = q_ref.shape[0] // TILE
    slots = kbuf.shape[0] // TILE
    me = lax.axis_index("dim")
    fact = lax.axis_index("fact")
    mesh = pl.DeviceIdType.MESH
    for hp in range(pairs):
        cols = pl.ds(hp * PAIR, PAIR)
        for peer in range(owners):
            chosen = pick_ref[peer]
            stage[hp, peer, 0] = k_ref[chosen, :, cols]
            stage[hp, peer, 1] = v_ref[chosen, :, cols]
    for hp in range(pairs):
        recv[hp][me] = stage[hp, me]
    barrier = pltpu.get_barrier_semaphore()
    for k in range(1, owners):
        pl.semaphore_signal(barrier, inc=1, device_id=(fact, lax.rem(me + k, owners)), device_id_type=mesh)
    pl.semaphore_wait(barrier, owners - 1)

    def remote(hp, k, src):
        dest = lax.rem(me + k, owners)
        return pltpu.make_async_remote_copy(
            src_ref=stage.at[hp, dest],
            dst_ref=recv[hp].at[src],
            send_sem=send_sem.at[hp, dest],
            recv_sem=recv_sem.at[hp, src],
            device_id=(fact, dest),
            device_id_type=mesh,
        )

    for hp in range(pairs):
        for k in range(1, owners):
            remote(hp, k, me).start()

    gbuf[:, slots] = jnp.zeros(gbuf.shape[:1] + gbuf.shape[2:], gbuf.dtype)
    lane = lax.broadcasted_iota(jnp.int32, (1, PAIR), 1)
    first = lane < HEAD_DIM
    key_pos = lax.broadcasted_iota(jnp.int32, (1, slots * TILE), 1)
    for hp in range(pairs):
        cols = pl.ds(hp * PAIR, PAIR)
        for k in range(1, owners):
            remote(hp, owners - k, lax.rem(me + k, owners)).wait_recv()
        for t in range(tiles):
            rows = pl.ds(t * TILE, TILE)
            for j in range(slots):
                owner = owner_ref[t, j]
                kbuf[pl.ds(j * TILE, TILE), :] = recv[hp][owner, 0]
                vbuf[pl.ds(j * TILE, TILE), :] = recv[hp][owner, 1]
            alive = key_pos < length_ref[t] * TILE
            attended, query_grad, key_grad, value_grad = pair_attention(
                q_ref[rows, cols], g_ref[rows, cols], kbuf[...], vbuf[...], alive, first
            )
            att_ref[rows, cols] = attended.astype(att_ref.dtype)
            qg_ref[rows, cols] = query_grad.astype(qg_ref.dtype)
            for j in range(slots):
                gbuf[t, j, :, :PAIR] = key_grad[j * TILE:(j + 1) * TILE]
                gbuf[t, j, :, PAIR:] = value_grad[j * TILE:(j + 1) * TILE]
        for owner in range(owners):
            total = gbuf[0, slot_ref[0, owner]]
            for t in range(1, tiles):
                total = total + gbuf[t, slot_ref[t, owner]]
            grad_ref[hp, owner] = total.astype(grad_ref.dtype)
    for hp in range(pairs):
        for k in range(1, owners):
            remote(hp, k, me).wait_send()


def fetch_attend(picks, owner_of, tile_lengths, slot_of, key_blocks, value_blocks, queries, cotangent):
    _, _, width = key_blocks.shape
    owners = picks.shape[0]
    rows = queries.shape[0]
    slots = owner_of.shape[1]
    pairs = width // PAIR
    whole = pl.BlockSpec(memory_space=pltpu.VMEM)
    grid_spec = pltpu.PrefetchScalarGridSpec(
        num_scalar_prefetch=4,
        grid=(1,),
        in_specs=[whole] * 4,
        out_specs=[whole] * 3,
        scratch_shapes=[
            pltpu.VMEM((pairs, owners, 2, TILE, PAIR), jnp.bfloat16),
            pltpu.VMEM((slots * TILE, PAIR), jnp.bfloat16),
            pltpu.VMEM((slots * TILE, PAIR), jnp.bfloat16),
            pltpu.VMEM((rows // TILE, slots + 1, TILE, 2 * PAIR), jnp.float32),
            pltpu.SemaphoreType.DMA((pairs, owners)),
            pltpu.SemaphoreType.DMA((pairs, owners)),
        ] + [pltpu.VMEM((owners, 2, TILE, PAIR), jnp.bfloat16) for _ in range(pairs)],
    )
    return pl.pallas_call(
        fetch_attend_kernel,
        grid_spec=grid_spec,
        out_shape=[
            jax.ShapeDtypeStruct((rows, width), jnp.bfloat16),
            jax.ShapeDtypeStruct((rows, width), jnp.bfloat16),
            jax.ShapeDtypeStruct((pairs, owners, TILE, 2 * PAIR), jnp.bfloat16),
        ],
        compiler_params=pltpu.CompilerParams(
            collective_id=0, has_side_effects=True, vmem_limit_bytes=60 * 1024 * 1024
        ),
    )(picks, owner_of, tile_lengths, slot_of, key_blocks, value_blocks, queries, cotangent)


def sum_kernel(req_ref, piece_ref, key_out, value_out, acc):
    step = pl.program_id(0)
    chunk = piece_ref.shape[0]
    span = key_out.shape[1]
    rows = piece_ref.shape[1]

    @pl.when(step == 0)
    def _():
        acc[...] = jnp.zeros_like(acc)

    for i in range(chunk):
        target = req_ref[step * chunk + i]

        @pl.when(target >= 0)
        def _():
            acc[target] = acc[target] + piece_ref[i].astype(jnp.float32)

    @pl.when(step == pl.num_programs(0) - 1)
    def _():
        for l in range(acc.shape[0]):
            key_out[pl.ds(l * rows, rows), :] = acc[l, :, :span].astype(key_out.dtype)
            value_out[pl.ds(l * rows, rows), :] = acc[l, :, span:].astype(value_out.dtype)


def sum_pieces(all_requests, pieces, blocks):
    sources, rows, both = pieces.shape
    span = both // 2
    chunk = 16
    grid_spec = pltpu.PrefetchScalarGridSpec(
        num_scalar_prefetch=1,
        grid=(sources // chunk,),
        in_specs=[pl.BlockSpec((chunk, rows, both), lambda i, req: (i, 0, 0))],
        out_specs=[
            pl.BlockSpec((blocks * rows, span), lambda i, req: (0, 0)),
            pl.BlockSpec((blocks * rows, span), lambda i, req: (0, 0)),
        ],
        scratch_shapes=[pltpu.VMEM((blocks, rows, both), jnp.float32)],
    )
    return pl.pallas_call(
        sum_kernel,
        grid_spec=grid_spec,
        out_shape=[
            jax.ShapeDtypeStruct((blocks * rows, span), jnp.bfloat16),
            jax.ShapeDtypeStruct((blocks * rows, span), jnp.bfloat16),
        ],
        compiler_params=pltpu.CompilerParams(dimension_semantics=("arbitrary",)),
    )(all_requests, pieces)


def body(queries, key_rows, value_rows, cotangent, block_lists, tile_lengths):
    owners = lax.axis_size("dim")
    tile_count = block_lists.shape[0]
    slot_count = block_lists.shape[1]
    blocks_here = key_rows.shape[0] // TILE
    model_width = key_rows.shape[1]
    alive_slots = jnp.arange(slot_count, dtype=jnp.int32)[None, :] < tile_lengths[:, None]
    owner_of = jnp.clip(block_lists // blocks_here, 0, owners - 1)
    local_of = block_lists % blocks_here
    owner_ids = jnp.arange(owners, dtype=jnp.int32)
    matched = (owner_of[:, :, None] == owner_ids[None, None, :]) & alive_slots[:, :, None]
    wanted = jnp.max(jnp.where(matched, local_of[:, :, None], -1), axis=(0, 1))
    everyone = lax.all_gather(wanted, ("fact", "dim"), tiled=False)
    me = lax.axis_index("dim")
    fact = lax.axis_index("fact")
    column = lax.dynamic_slice_in_dim(everyone, me, 1, axis=1).reshape(everyone.shape[0])
    requests = lax.dynamic_slice_in_dim(column, fact * owners, owners)
    block_ids = jnp.arange(blocks_here, dtype=jnp.int32)[None, :]
    picks = jnp.clip(requests, 0, blocks_here - 1)
    slot_ids = jnp.arange(slot_count, dtype=jnp.int32)[None, :, None]
    live_match = (owner_of[:, :, None] == owner_ids[None, None, :]) & alive_slots[:, :, None]
    slot_of = jnp.min(jnp.where(live_match, slot_ids, slot_count), axis=1)
    attended_out, query_grad_out, partial_grads = fetch_attend(
        picks,
        owner_of,
        tile_lengths,
        slot_of,
        key_rows.reshape(blocks_here, TILE, model_width),
        value_rows.reshape(blocks_here, TILE, model_width),
        queries,
        cotangent,
    )
    fact_count = lax.axis_size("fact")
    span = model_width // fact_count
    pieces = lax.all_to_all(
        partial_grads.reshape(fact_count * owners, TILE, 2 * span),
        ("fact", "dim"), split_axis=0, concat_axis=0, tiled=True,
    )
    all_requests = column
    key_grad_out, value_grad_out = sum_pieces(all_requests, pieces, blocks_here)
    return (
        attended_out,
        query_grad_out,
        key_grad_out,
        value_grad_out,
    )


def solution(mesh):
    in_specs = (
        P(("fact", "dim"), None),
        P("dim", None),
        P("dim", None),
        P(("fact", "dim"), None),
        P(("fact", "dim"), None),
        P(("fact", "dim")),
    )
    out_specs = (
        P(("fact", "dim"), None),
        P(("fact", "dim"), None),
        P("dim", "fact"),
        P("dim", "fact"),
    )
    return jax.shard_map(body, mesh=mesh, in_specs=in_specs, out_specs=out_specs, check_vma=False)
```

```python
import functools
import jax
import jax.numpy as jnp
from jax import lax
from jax.experimental import pallas as pl
from jax.experimental.pallas import tpu as pltpu
from jax.sharding import PartitionSpec as P

HEADS = 16
HEAD_DIM = 64
TILE = 128
NEG_FILL = -1e30
PAIR = 2 * HEAD_DIM


def _nt(a, b):
    return lax.dot_general(a, b, (((1,), (1,)), ((), ())), preferred_element_type=jnp.float32)


def _tn(a, b):
    return lax.dot_general(a, b, (((0,), (0,)), ((), ())), preferred_element_type=jnp.float32)


def _nn(a, b):
    return jnp.dot(a, b, preferred_element_type=jnp.float32)


def pair_attention(q, g, keys, values, alive, first):
    scale = HEAD_DIM ** (-0.5)
    outs = []
    for h in range(2):
        mine = first if h == 0 else jnp.logical_not(first)
        qh = jnp.where(mine, q, jnp.zeros_like(q))
        gh = jnp.where(mine, g, jnp.zeros_like(g))
        scores = _nt(qh, keys) * scale
        scores = jnp.where(alive, scores, NEG_FILL)
        row_max = jnp.max(scores, axis=-1, keepdims=True)
        expo = jnp.exp(scores - row_max)
        weights = expo / jnp.sum(expo, axis=-1, keepdims=True)
        weights_low = weights.astype(jnp.bfloat16)
        attended = _nn(weights_low, values)
        dweights = _nt(gh, values)
        row_delta = jnp.sum(weights * dweights, axis=-1, keepdims=True)
        dscores = (weights * (dweights - row_delta)).astype(jnp.bfloat16)
        query_grad = _nn(dscores, keys)
        key_grad = _tn(dscores, q)
        value_grad = _tn(weights_low, g)
        outs.append((attended, query_grad, key_grad, value_grad))
    pick = lambda i: jnp.where(first, outs[0][i], outs[1][i])
    return pick(0), pick(1) * scale, pick(2) * scale, pick(3)


def fetch_attend_kernel(pick_ref, owner_ref, length_ref, slot_ref, k_ref, v_ref, q_ref, g_ref,
                        att_ref, qg_ref, kgrad_ref, vgrad_ref,
                        stage, kbuf, vbuf, gbuf, gsend, send_sem, recv_sem, out_sem, *recv):
    owners = stage.shape[1]
    pairs = stage.shape[0]
    tiles = q_ref.shape[0] // TILE
    slots = kbuf.shape[0] // TILE
    me = lax.axis_index("dim")
    fact = lax.axis_index("fact")
    mesh = pl.DeviceIdType.MESH
    for hp in range(pairs):
        cols = pl.ds(hp * PAIR, PAIR)
        for peer in range(owners):
            chosen = pick_ref[peer]
            stage[hp, peer, 0] = k_ref[chosen, :, cols]
            stage[hp, peer, 1] = v_ref[chosen, :, cols]
    for hp in range(pairs):
        recv[hp][me] = stage[hp, me]
    barrier = pltpu.get_barrier_semaphore()
    for k in range(1, owners):
        pl.semaphore_signal(barrier, inc=1, device_id=(fact, lax.rem(me + k, owners)), device_id_type=mesh)
    pl.semaphore_wait(barrier, owners - 1)

    def remote(hp, k, src):
        dest = lax.rem(me + k, owners)
        return pltpu.make_async_remote_copy(
            src_ref=stage.at[hp, dest],
            dst_ref=recv[hp].at[src],
            send_sem=send_sem.at[hp, dest],
            recv_sem=recv_sem.at[hp, src],
            device_id=(fact, dest),
            device_id_type=mesh,
        )

    for hp in range(pairs):
        for k in range(1, owners):
            remote(hp, k, me).start()

    gbuf[:, slots] = jnp.zeros(gbuf.shape[:1] + gbuf.shape[2:], gbuf.dtype)
    lane = lax.broadcasted_iota(jnp.int32, (1, PAIR), 1)
    first = lane < HEAD_DIM
    key_pos = lax.broadcasted_iota(jnp.int32, (1, slots * TILE), 1)
    for hp in range(pairs):
        cols = pl.ds(hp * PAIR, PAIR)
        for k in range(1, owners):
            remote(hp, owners - k, lax.rem(me + k, owners)).wait_recv()
        for t in range(tiles):
            rows = pl.ds(t * TILE, TILE)
            for j in range(slots):
                owner = owner_ref[t, j]
                kbuf[pl.ds(j * TILE, TILE), :] = recv[hp][owner, 0]
                vbuf[pl.ds(j * TILE, TILE), :] = recv[hp][owner, 1]
            alive = key_pos < length_ref[t] * TILE
            attended, query_grad, key_grad, value_grad = pair_attention(
                q_ref[rows, cols], g_ref[rows, cols], kbuf[...], vbuf[...], alive, first
            )
            att_ref[rows, cols] = attended.astype(att_ref.dtype)
            qg_ref[rows, cols] = query_grad.astype(qg_ref.dtype)
            for j in range(slots):
                gbuf[t, j, :, :PAIR] = key_grad[j * TILE:(j + 1) * TILE]
                gbuf[t, j, :, PAIR:] = value_grad[j * TILE:(j + 1) * TILE]
        for owner in range(owners):
            total = gbuf[0, slot_ref[0, owner]]
            for t in range(1, tiles):
                total = total + gbuf[t, slot_ref[t, owner]]
            gsend[hp, owner, 0] = total[:, :PAIR].astype(gsend.dtype)
            gsend[hp, owner, 1] = total[:, PAIR:].astype(gsend.dtype)
        for plane, dst in enumerate((kgrad_ref, vgrad_ref)):
            pltpu.make_async_copy(gsend.at[hp, :, plane], dst.at[hp], out_sem.at[hp, plane]).start()
    for hp in range(pairs):
        for k in range(1, owners):
            remote(hp, k, me).wait_send()
        for plane, dst in enumerate((kgrad_ref, vgrad_ref)):
            pltpu.make_async_copy(gsend.at[hp, :, plane], dst.at[hp], out_sem.at[hp, plane]).wait()


def fetch_attend(picks, owner_of, tile_lengths, slot_of, key_blocks, value_blocks, queries, cotangent):
    _, _, width = key_blocks.shape
    owners = picks.shape[0]
    rows = queries.shape[0]
    slots = owner_of.shape[1]
    pairs = width // PAIR
    whole = pl.BlockSpec(memory_space=pltpu.VMEM)
    grid_spec = pltpu.PrefetchScalarGridSpec(
        num_scalar_prefetch=4,
        grid=(1,),
        in_specs=[whole] * 4,
        out_specs=[whole, whole, pl.BlockSpec(memory_space=pl.ANY), pl.BlockSpec(memory_space=pl.ANY)],
        scratch_shapes=[
            pltpu.VMEM((pairs, owners, 2, TILE, PAIR), jnp.bfloat16),
            pltpu.VMEM((slots * TILE, PAIR), jnp.bfloat16),
            pltpu.VMEM((slots * TILE, PAIR), jnp.bfloat16),
            pltpu.VMEM((rows // TILE, slots + 1, TILE, 2 * PAIR), jnp.float32),
            pltpu.VMEM((pairs, owners, 2, TILE, PAIR), jnp.bfloat16),
            pltpu.SemaphoreType.DMA((pairs, owners)),
            pltpu.SemaphoreType.DMA((pairs, owners)),
            pltpu.SemaphoreType.DMA((pairs, 2)),
        ] + [pltpu.VMEM((owners, 2, TILE, PAIR), jnp.bfloat16) for _ in range(pairs)],
    )
    return pl.pallas_call(
        fetch_attend_kernel,
        grid_spec=grid_spec,
        out_shape=[
            jax.ShapeDtypeStruct((rows, width), jnp.bfloat16),
            jax.ShapeDtypeStruct((rows, width), jnp.bfloat16),
            jax.ShapeDtypeStruct((pairs, owners, TILE, PAIR), jnp.bfloat16),
            jax.ShapeDtypeStruct((pairs, owners, TILE, PAIR), jnp.bfloat16),
        ],
        compiler_params=pltpu.CompilerParams(
            collective_id=0, has_side_effects=True, vmem_limit_bytes=60 * 1024 * 1024
        ),
    )(picks, owner_of, tile_lengths, slot_of, key_blocks, value_blocks, queries, cotangent)


def sum_kernel(req_ref, piece_ref, out_ref, acc):
    step = pl.program_id(0)
    chunk = piece_ref.shape[0]
    rows = piece_ref.shape[1]

    @pl.when(step == 0)
    def _():
        acc[...] = jnp.zeros_like(acc)

    for i in range(chunk):
        target = req_ref[step * chunk + i]

        @pl.when(target >= 0)
        def _():
            acc[target] = acc[target] + piece_ref[i].astype(jnp.float32)

    @pl.when(step == pl.num_programs(0) - 1)
    def _():
        for l in range(acc.shape[0]):
            out_ref[pl.ds(l * rows, rows), :] = acc[l].astype(out_ref.dtype)


def sum_pieces(all_requests, pieces, blocks):
    sources, rows, span = pieces.shape
    chunk = 16
    grid_spec = pltpu.PrefetchScalarGridSpec(
        num_scalar_prefetch=1,
        grid=(sources // chunk,),
        in_specs=[pl.BlockSpec((chunk, rows, span), lambda i, req: (i, 0, 0))],
        out_specs=pl.BlockSpec((blocks * rows, span), lambda i, req: (0, 0)),
        scratch_shapes=[pltpu.VMEM((blocks, rows, span), jnp.float32)],
    )
    return pl.pallas_call(
        sum_kernel,
        grid_spec=grid_spec,
        out_shape=jax.ShapeDtypeStruct((blocks * rows, span), jnp.bfloat16),
        compiler_params=pltpu.CompilerParams(dimension_semantics=("arbitrary",)),
    )(all_requests, pieces)


def body(queries, key_rows, value_rows, cotangent, block_lists, tile_lengths):
    owners = lax.axis_size("dim")
    tile_count = block_lists.shape[0]
    slot_count = block_lists.shape[1]
    blocks_here = key_rows.shape[0] // TILE
    model_width = key_rows.shape[1]
    alive_slots = jnp.arange(slot_count, dtype=jnp.int32)[None, :] < tile_lengths[:, None]
    owner_of = jnp.clip(block_lists // blocks_here, 0, owners - 1)
    local_of = block_lists % blocks_here
    owner_ids = jnp.arange(owners, dtype=jnp.int32)
    matched = (owner_of[:, :, None] == owner_ids[None, None, :]) & alive_slots[:, :, None]
    wanted = jnp.max(jnp.where(matched, local_of[:, :, None], -1), axis=(0, 1))
    requests = lax.all_to_all(
        wanted.reshape(owners, 1), "dim", split_axis=0, concat_axis=0, tiled=True
    )
    block_ids = jnp.arange(blocks_here, dtype=jnp.int32)[None, :]
    picks = jnp.clip(requests.reshape(owners), 0, blocks_here - 1)
    slot_ids = jnp.arange(slot_count, dtype=jnp.int32)[None, :, None]
    live_match = (owner_of[:, :, None] == owner_ids[None, None, :]) & alive_slots[:, :, None]
    slot_of = jnp.min(jnp.where(live_match, slot_ids, slot_count), axis=1)
    attended_out, query_grad_out, key_parts, value_parts = fetch_attend(
        picks,
        owner_of,
        tile_lengths,
        slot_of,
        key_rows.reshape(blocks_here, TILE, model_width),
        value_rows.reshape(blocks_here, TILE, model_width),
        queries,
        cotangent,
    )
    fact_count = lax.axis_size("fact")
    span = model_width // fact_count
    all_requests = lax.all_gather(requests.reshape(owners), "fact", tiled=True)
    key_pieces = lax.all_to_all(
        key_parts.reshape(fact_count * owners, TILE, span),
        ("fact", "dim"), split_axis=0, concat_axis=0, tiled=True,
    )
    key_grad_out = sum_pieces(all_requests, key_pieces, blocks_here)
    value_pieces = lax.all_to_all(
        value_parts.reshape(fact_count * owners, TILE, span),
        ("fact", "dim"), split_axis=0, concat_axis=0, tiled=True,
    )
    value_grad_out = sum_pieces(all_requests, value_pieces, blocks_here)
    return (
        attended_out,
        query_grad_out,
        key_grad_out,
        value_grad_out,
    )


def solution(mesh):
    in_specs = (
        P(("fact", "dim"), None),
        P("dim", None),
        P("dim", None),
        P(("fact", "dim"), None),
        P(("fact", "dim"), None),
        P(("fact", "dim")),
    )
    out_specs = (
        P(("fact", "dim"), None),
        P(("fact", "dim"), None),
        P("dim", "fact"),
        P("dim", "fact"),
    )
    return jax.shard_map(body, mesh=mesh, in_specs=in_specs, out_specs=out_specs, check_vma=False)
```

```python
import functools
import jax
import jax.numpy as jnp
from jax import lax
from jax.experimental import pallas as pl
from jax.experimental.pallas import tpu as pltpu
from jax.sharding import PartitionSpec as P

HEADS = 16
HEAD_DIM = 64
TILE = 128
NEG_FILL = -1e30
PAIR = 2 * HEAD_DIM


def _nt(a, b):
    return lax.dot_general(a, b, (((1,), (1,)), ((), ())), preferred_element_type=jnp.float32)


def _tn(a, b):
    return lax.dot_general(a, b, (((0,), (0,)), ((), ())), preferred_element_type=jnp.float32)


def _nn(a, b):
    return jnp.dot(a, b, preferred_element_type=jnp.float32)


def pair_attention(q, g, keys, values, alive, first):
    scale = HEAD_DIM ** (-0.5)
    outs = []
    for h in range(2):
        mine = first if h == 0 else jnp.logical_not(first)
        qh = jnp.where(mine, q, jnp.zeros_like(q))
        gh = jnp.where(mine, g, jnp.zeros_like(g))
        scores = _nt(qh, keys) * scale
        scores = jnp.where(alive, scores, NEG_FILL)
        row_max = jnp.max(scores, axis=-1, keepdims=True)
        expo = jnp.exp(scores - row_max)
        weights = expo / jnp.sum(expo, axis=-1, keepdims=True)
        weights_low = weights.astype(jnp.bfloat16)
        attended = _nn(weights_low, values)
        dweights = _nt(gh, values)
        row_delta = jnp.sum(weights * dweights, axis=-1, keepdims=True)
        dscores = (weights * (dweights - row_delta)).astype(jnp.bfloat16)
        query_grad = _nn(dscores, keys)
        key_grad = _tn(dscores, q)
        value_grad = _tn(weights_low, g)
        outs.append((attended, query_grad, key_grad, value_grad))
    pick = lambda i: jnp.where(first, outs[0][i], outs[1][i])
    return pick(0), pick(1) * scale, pick(2) * scale, pick(3)


def fetch_attend_kernel(pick_ref, owner_ref, length_ref, slot_ref, k_ref, v_ref, q_ref, g_ref,
                        att_ref, qg_ref, grad_ref,
                        stage, kbuf, vbuf, gbuf, send_sem, recv_sem, *recv):
    owners = stage.shape[1]
    pairs = stage.shape[0]
    tiles = q_ref.shape[0] // TILE
    slots = kbuf.shape[0] // TILE
    me = lax.axis_index("dim")
    fact = lax.axis_index("fact")
    mesh = pl.DeviceIdType.MESH
    for hp in range(pairs):
        cols = pl.ds(hp * PAIR, PAIR)
        for peer in range(owners):
            chosen = pick_ref[peer]
            stage[hp, peer, 0] = k_ref[chosen, :, cols]
            stage[hp, peer, 1] = v_ref[chosen, :, cols]
    for hp in range(pairs):
        recv[hp][me] = stage[hp, me]
    barrier = pltpu.get_barrier_semaphore()
    for k in range(1, owners):
        pl.semaphore_signal(barrier, inc=1, device_id=(fact, lax.rem(me + k, owners)), device_id_type=mesh)
    pl.semaphore_wait(barrier, owners - 1)

    def remote(hp, k, src):
        dest = lax.rem(me + k, owners)
        return pltpu.make_async_remote_copy(
            src_ref=stage.at[hp, dest],
            dst_ref=recv[hp].at[src],
            send_sem=send_sem.at[hp, dest],
            recv_sem=recv_sem.at[hp, src],
            device_id=(fact, dest),
            device_id_type=mesh,
        )

    for hp in range(pairs):
        for k in range(1, owners):
            remote(hp, k, me).start()

    gbuf[:, slots] = jnp.zeros(gbuf.shape[:1] + gbuf.shape[2:], gbuf.dtype)
    lane = lax.broadcasted_iota(jnp.int32, (1, PAIR), 1)
    first = lane < HEAD_DIM
    key_pos = lax.broadcasted_iota(jnp.int32, (1, slots * TILE), 1)
    for hp in range(pairs):
        cols = pl.ds(hp * PAIR, PAIR)
        for k in range(1, owners):
            remote(hp, owners - k, lax.rem(me + k, owners)).wait_recv()
        for t in range(tiles):
            rows = pl.ds(t * TILE, TILE)
            for j in range(slots):
                owner = owner_ref[t, j]
                kbuf[pl.ds(j * TILE, TILE), :] = recv[hp][owner, 0]
                vbuf[pl.ds(j * TILE, TILE), :] = recv[hp][owner, 1]
            alive = key_pos < length_ref[t] * TILE
            attended, query_grad, key_grad, value_grad = pair_attention(
                q_ref[rows, cols], g_ref[rows, cols], kbuf[...], vbuf[...], alive, first
            )
            att_ref[rows, cols] = attended.astype(att_ref.dtype)
            qg_ref[rows, cols] = query_grad.astype(qg_ref.dtype)
            for j in range(slots):
                gbuf[t, j, :, :PAIR] = key_grad[j * TILE:(j + 1) * TILE]
                gbuf[t, j, :, PAIR:] = value_grad[j * TILE:(j + 1) * TILE]
        for owner in range(owners):
            total = gbuf[0, slot_ref[0, owner]]
            for t in range(1, tiles):
                total = total + gbuf[t, slot_ref[t, owner]]
            grad_ref[hp, owner] = total.astype(grad_ref.dtype)
    for hp in range(pairs):
        for k in range(1, owners):
            remote(hp, k, me).wait_send()


def fetch_attend(picks, owner_of, tile_lengths, slot_of, key_blocks, value_blocks, queries, cotangent):
    _, _, width = key_blocks.shape
    owners = picks.shape[0]
    rows = queries.shape[0]
    slots = owner_of.shape[1]
    pairs = width // PAIR
    whole = pl.BlockSpec(memory_space=pltpu.VMEM)
    grid_spec = pltpu.PrefetchScalarGridSpec(
        num_scalar_prefetch=4,
        grid=(1,),
        in_specs=[whole] * 4,
        out_specs=[whole] * 3,
        scratch_shapes=[
            pltpu.VMEM((pairs, owners, 2, TILE, PAIR), jnp.bfloat16),
            pltpu.VMEM((slots * TILE, PAIR), jnp.bfloat16),
            pltpu.VMEM((slots * TILE, PAIR), jnp.bfloat16),
            pltpu.VMEM((rows // TILE, slots + 1, TILE, 2 * PAIR), jnp.float32),
            pltpu.SemaphoreType.DMA((pairs, owners)),
            pltpu.SemaphoreType.DMA((pairs, owners)),
        ] + [pltpu.VMEM((owners, 2, TILE, PAIR), jnp.bfloat16) for _ in range(pairs)],
    )
    return pl.pallas_call(
        fetch_attend_kernel,
        grid_spec=grid_spec,
        out_shape=[
            jax.ShapeDtypeStruct((rows, width), jnp.bfloat16),
            jax.ShapeDtypeStruct((rows, width), jnp.bfloat16),
            jax.ShapeDtypeStruct((pairs, owners, TILE, 2 * PAIR), jnp.bfloat16),
        ],
        compiler_params=pltpu.CompilerParams(
            collective_id=0, has_side_effects=True, vmem_limit_bytes=60 * 1024 * 1024
        ),
    )(picks, owner_of, tile_lengths, slot_of, key_blocks, value_blocks, queries, cotangent)


def sum_kernel(req_ref, piece_ref, key_out, value_out, acc):
    step = pl.program_id(0)
    chunk = piece_ref.shape[0]
    span = key_out.shape[1]
    rows = piece_ref.shape[1]

    @pl.when(step == 0)
    def _():
        acc[...] = jnp.zeros_like(acc)

    spare = acc.shape[0] - 1
    for i in range(chunk):
        target = req_ref[step * chunk + i]
        target = jnp.where(target < 0, spare, jnp.minimum(target, spare))
        acc[target] = acc[target] + piece_ref[i].astype(jnp.float32)

    @pl.when(step == pl.num_programs(0) - 1)
    def _():
        for l in range(acc.shape[0] - 1):
            key_out[pl.ds(l * rows, rows), :] = acc[l, :, :span].astype(key_out.dtype)
            value_out[pl.ds(l * rows, rows), :] = acc[l, :, span:].astype(value_out.dtype)


def sum_pieces(all_requests, pieces, blocks):
    sources, rows, both = pieces.shape
    span = both // 2
    chunk = 32
    grid_spec = pltpu.PrefetchScalarGridSpec(
        num_scalar_prefetch=1,
        grid=(sources // chunk,),
        in_specs=[pl.BlockSpec((chunk, rows, both), lambda i, req: (i, 0, 0))],
        out_specs=[
            pl.BlockSpec((blocks * rows, span), lambda i, req: (0, 0)),
            pl.BlockSpec((blocks * rows, span), lambda i, req: (0, 0)),
        ],
        scratch_shapes=[pltpu.VMEM((blocks + 1, rows, both), jnp.float32)],
    )
    return pl.pallas_call(
        sum_kernel,
        grid_spec=grid_spec,
        out_shape=[
            jax.ShapeDtypeStruct((blocks * rows, span), jnp.bfloat16),
            jax.ShapeDtypeStruct((blocks * rows, span), jnp.bfloat16),
        ],
        compiler_params=pltpu.CompilerParams(dimension_semantics=("arbitrary",)),
    )(all_requests, pieces)


def body(queries, key_rows, value_rows, cotangent, block_lists, tile_lengths):
    owners = lax.axis_size("dim")
    tile_count = block_lists.shape[0]
    slot_count = block_lists.shape[1]
    blocks_here = key_rows.shape[0] // TILE
    model_width = key_rows.shape[1]
    alive_slots = jnp.arange(slot_count, dtype=jnp.int32)[None, :] < tile_lengths[:, None]
    owner_of = jnp.clip(block_lists // blocks_here, 0, owners - 1)
    local_of = block_lists % blocks_here
    owner_ids = jnp.arange(owners, dtype=jnp.int32)
    matched = (owner_of[:, :, None] == owner_ids[None, None, :]) & alive_slots[:, :, None]
    wanted = jnp.max(jnp.where(matched, local_of[:, :, None], -1), axis=(0, 1))
    requests = lax.all_to_all(
        wanted.reshape(owners, 1), "dim", split_axis=0, concat_axis=0, tiled=True
    )
    block_ids = jnp.arange(blocks_here, dtype=jnp.int32)[None, :]
    picks = jnp.clip(requests.reshape(owners), 0, blocks_here - 1)
    slot_ids = jnp.arange(slot_count, dtype=jnp.int32)[None, :, None]
    live_match = (owner_of[:, :, None] == owner_ids[None, None, :]) & alive_slots[:, :, None]
    slot_of = jnp.min(jnp.where(live_match, slot_ids, slot_count), axis=1)
    attended_out, query_grad_out, partial_grads = fetch_attend(
        picks,
        owner_of,
        tile_lengths,
        slot_of,
        key_rows.reshape(blocks_here, TILE, model_width),
        value_rows.reshape(blocks_here, TILE, model_width),
        queries,
        cotangent,
    )
    fact_count = lax.axis_size("fact")
    span = model_width // fact_count
    pieces = lax.all_to_all(
        partial_grads.reshape(fact_count * owners, TILE, 2 * span),
        ("fact", "dim"), split_axis=0, concat_axis=0, tiled=True,
    )
    all_requests = lax.all_gather(requests.reshape(owners), "fact", tiled=True)
    key_grad_out, value_grad_out = sum_pieces(all_requests, pieces, blocks_here)
    return (
        attended_out,
        query_grad_out,
        key_grad_out,
        value_grad_out,
    )


def solution(mesh):
    in_specs = (
        P(("fact", "dim"), None),
        P("dim", None),
        P("dim", None),
        P(("fact", "dim"), None),
        P(("fact", "dim"), None),
        P(("fact", "dim")),
    )
    out_specs = (
        P(("fact", "dim"), None),
        P(("fact", "dim"), None),
        P("dim", "fact"),
        P("dim", "fact"),
    )
    return jax.shard_map(body, mesh=mesh, in_specs=in_specs, out_specs=out_specs, check_vma=False)
```

```python
import functools
import jax
import jax.numpy as jnp
from jax import lax
from jax.experimental import pallas as pl
from jax.experimental.pallas import tpu as pltpu
from jax.sharding import PartitionSpec as P

HEADS = 16
HEAD_DIM = 64
TILE = 128
NEG_FILL = -1e30
PAIR = 2 * HEAD_DIM


def _nt(a, b):
    return lax.dot_general(a, b, (((1,), (1,)), ((), ())), preferred_element_type=jnp.float32)


def _tn(a, b):
    return lax.dot_general(a, b, (((0,), (0,)), ((), ())), preferred_element_type=jnp.float32)


def _nn(a, b):
    return jnp.dot(a, b, preferred_element_type=jnp.float32)


def pair_attention(q, g, keys, values, alive, first):
    scale = HEAD_DIM ** (-0.5)
    outs = []
    for h in range(2):
        mine = first if h == 0 else jnp.logical_not(first)
        qh = jnp.where(mine, q, jnp.zeros_like(q))
        gh = jnp.where(mine, g, jnp.zeros_like(g))
        scores = _nt(qh, keys) * scale
        scores = jnp.where(alive, scores, NEG_FILL)
        row_max = jnp.max(scores, axis=-1, keepdims=True)
        expo = jnp.exp(scores - row_max)
        weights = expo / jnp.sum(expo, axis=-1, keepdims=True)
        weights_low = weights.astype(jnp.bfloat16)
        attended = _nn(weights_low, values)
        dweights = _nt(gh, values)
        row_delta = jnp.sum(weights * dweights, axis=-1, keepdims=True)
        dscores = (weights * (dweights - row_delta)).astype(jnp.bfloat16)
        query_grad = _nn(dscores, keys)
        key_grad = _tn(dscores, q)
        value_grad = _tn(weights_low, g)
        outs.append((attended, query_grad, key_grad, value_grad))
    pick = lambda i: jnp.where(first, outs[0][i], outs[1][i])
    return pick(0), pick(1) * scale, pick(2) * scale, pick(3)


def fetch_attend_kernel(pick_ref, owner_ref, length_ref, slot_ref, k_ref, v_ref, q_ref, g_ref,
                        att_ref, qg_ref, grad_ref,
                        stage, kbuf, vbuf, gbuf, gsend, send_sem, recv_sem, out_sem, *recv):
    owners = stage.shape[1]
    pairs = stage.shape[0]
    tiles = q_ref.shape[0] // TILE
    slots = kbuf.shape[0] // TILE
    me = lax.axis_index("dim")
    fact = lax.axis_index("fact")
    mesh = pl.DeviceIdType.MESH
    for hp in range(pairs):
        cols = pl.ds(hp * PAIR, PAIR)
        for peer in range(owners):
            chosen = pick_ref[peer]
            stage[hp, peer, 0] = k_ref[chosen, :, cols]
            stage[hp, peer, 1] = v_ref[chosen, :, cols]
    for hp in range(pairs):
        recv[hp][me] = stage[hp, me]
    barrier = pltpu.get_barrier_semaphore()
    for k in range(1, owners):
        pl.semaphore_signal(barrier, inc=1, device_id=(fact, lax.rem(me + k, owners)), device_id_type=mesh)
    pl.semaphore_wait(barrier, owners - 1)

    def remote(hp, k, src):
        dest = lax.rem(me + k, owners)
        return pltpu.make_async_remote_copy(
            src_ref=stage.at[hp, dest],
            dst_ref=recv[hp].at[src],
            send_sem=send_sem.at[hp, dest],
            recv_sem=recv_sem.at[hp, src],
            device_id=(fact, dest),
            device_id_type=mesh,
        )

    for hp in range(pairs):
        for k in range(1, owners):
            remote(hp, k, me).start()

    gbuf[:, slots] = jnp.zeros(gbuf.shape[:1] + gbuf.shape[2:], gbuf.dtype)
    lane = lax.broadcasted_iota(jnp.int32, (1, PAIR), 1)
    first = lane < HEAD_DIM
    key_pos = lax.broadcasted_iota(jnp.int32, (1, slots * TILE), 1)
    for hp in range(pairs):
        cols = pl.ds(hp * PAIR, PAIR)
        for k in range(1, owners):
            remote(hp, owners - k, lax.rem(me + k, owners)).wait_recv()
        for t in range(tiles):
            rows = pl.ds(t * TILE, TILE)
            for j in range(slots):
                owner = owner_ref[t, j]
                kbuf[pl.ds(j * TILE, TILE), :] = recv[hp][owner, 0]
                vbuf[pl.ds(j * TILE, TILE), :] = recv[hp][owner, 1]
            alive = key_pos < length_ref[t] * TILE
            attended, query_grad, key_grad, value_grad = pair_attention(
                q_ref[rows, cols], g_ref[rows, cols], kbuf[...], vbuf[...], alive, first
            )
            att_ref[rows, cols] = attended.astype(att_ref.dtype)
            qg_ref[rows, cols] = query_grad.astype(qg_ref.dtype)
            for j in range(slots):
                gbuf[t, j, :, :PAIR] = key_grad[j * TILE:(j + 1) * TILE]
                gbuf[t, j, :, PAIR:] = value_grad[j * TILE:(j + 1) * TILE]
        for owner in range(owners):
            total = gbuf[0, slot_ref[0, owner]]
            for t in range(1, tiles):
                total = total + gbuf[t, slot_ref[t, owner]]
            gsend[hp, owner] = total.astype(gsend.dtype)
        pltpu.make_async_copy(gsend.at[hp], grad_ref.at[hp], out_sem.at[hp]).start()
    for hp in range(pairs):
        for k in range(1, owners):
            remote(hp, k, me).wait_send()
        pltpu.make_async_copy(gsend.at[hp], grad_ref.at[hp], out_sem.at[hp]).wait()


def fetch_attend(picks, owner_of, tile_lengths, slot_of, key_blocks, value_blocks, queries, cotangent):
    _, _, width = key_blocks.shape
    owners = picks.shape[0]
    rows = queries.shape[0]
    slots = owner_of.shape[1]
    pairs = width // PAIR
    whole = pl.BlockSpec(memory_space=pltpu.VMEM)
    grid_spec = pltpu.PrefetchScalarGridSpec(
        num_scalar_prefetch=4,
        grid=(1,),
        in_specs=[whole] * 4,
        out_specs=[whole, whole, pl.BlockSpec(memory_space=pl.ANY)],
        scratch_shapes=[
            pltpu.VMEM((pairs, owners, 2, TILE, PAIR), jnp.bfloat16),
            pltpu.VMEM((slots * TILE, PAIR), jnp.bfloat16),
            pltpu.VMEM((slots * TILE, PAIR), jnp.bfloat16),
            pltpu.VMEM((rows // TILE, slots + 1, TILE, 2 * PAIR), jnp.float32),
            pltpu.VMEM((pairs, owners, TILE, 2 * PAIR), jnp.bfloat16),
            pltpu.SemaphoreType.DMA((pairs, owners)),
            pltpu.SemaphoreType.DMA((pairs, owners)),
            pltpu.SemaphoreType.DMA((pairs,)),
        ] + [pltpu.VMEM((owners, 2, TILE, PAIR), jnp.bfloat16) for _ in range(pairs)],
    )
    return pl.pallas_call(
        fetch_attend_kernel,
        grid_spec=grid_spec,
        out_shape=[
            jax.ShapeDtypeStruct((rows, width), jnp.bfloat16),
            jax.ShapeDtypeStruct((rows, width), jnp.bfloat16),
            jax.ShapeDtypeStruct((pairs, owners, TILE, 2 * PAIR), jnp.bfloat16),
        ],
        compiler_params=pltpu.CompilerParams(
            collective_id=0, has_side_effects=True, vmem_limit_bytes=60 * 1024 * 1024
        ),
    )(picks, owner_of, tile_lengths, slot_of, key_blocks, value_blocks, queries, cotangent)


def sum_kernel(req_ref, piece_ref, key_out, value_out, acc):
    step = pl.program_id(0)
    chunk = piece_ref.shape[0]
    span = key_out.shape[1]
    rows = piece_ref.shape[1]

    @pl.when(step == 0)
    def _():
        acc[...] = jnp.zeros_like(acc)

    spare = acc.shape[0] - 1
    for i in range(chunk):
        target = req_ref[step * chunk + i]
        target = jnp.where(target < 0, spare, jnp.minimum(target, spare))
        acc[target] = acc[target] + piece_ref[i].astype(jnp.float32)

    @pl.when(step == pl.num_programs(0) - 1)
    def _():
        for l in range(acc.shape[0] - 1):
            key_out[pl.ds(l * rows, rows), :] = acc[l, :, :span].astype(key_out.dtype)
            value_out[pl.ds(l * rows, rows), :] = acc[l, :, span:].astype(value_out.dtype)


def sum_pieces(all_requests, pieces, blocks):
    sources, rows, both = pieces.shape
    span = both // 2
    chunk = 32
    grid_spec = pltpu.PrefetchScalarGridSpec(
        num_scalar_prefetch=1,
        grid=(sources // chunk,),
        in_specs=[pl.BlockSpec((chunk, rows, both), lambda i, req: (i, 0, 0))],
        out_specs=[
            pl.BlockSpec((blocks * rows, span), lambda i, req: (0, 0)),
            pl.BlockSpec((blocks * rows, span), lambda i, req: (0, 0)),
        ],
        scratch_shapes=[pltpu.VMEM((blocks + 1, rows, both), jnp.float32)],
    )
    return pl.pallas_call(
        sum_kernel,
        grid_spec=grid_spec,
        out_shape=[
            jax.ShapeDtypeStruct((blocks * rows, span), jnp.bfloat16),
            jax.ShapeDtypeStruct((blocks * rows, span), jnp.bfloat16),
        ],
        compiler_params=pltpu.CompilerParams(dimension_semantics=("arbitrary",)),
    )(all_requests, pieces)


def body(queries, key_rows, value_rows, cotangent, block_lists, tile_lengths):
    owners = lax.axis_size("dim")
    tile_count = block_lists.shape[0]
    slot_count = block_lists.shape[1]
    blocks_here = key_rows.shape[0] // TILE
    model_width = key_rows.shape[1]
    alive_slots = jnp.arange(slot_count, dtype=jnp.int32)[None, :] < tile_lengths[:, None]
    owner_of = jnp.clip(block_lists // blocks_here, 0, owners - 1)
    local_of = block_lists % blocks_here
    owner_ids = jnp.arange(owners, dtype=jnp.int32)
    matched = (owner_of[:, :, None] == owner_ids[None, None, :]) & alive_slots[:, :, None]
    wanted = jnp.max(jnp.where(matched, local_of[:, :, None], -1), axis=(0, 1))
    requests = lax.all_to_all(
        wanted.reshape(owners, 1), "dim", split_axis=0, concat_axis=0, tiled=True
    )
    block_ids = jnp.arange(blocks_here, dtype=jnp.int32)[None, :]
    picks = jnp.clip(requests.reshape(owners), 0, blocks_here - 1)
    slot_ids = jnp.arange(slot_count, dtype=jnp.int32)[None, :, None]
    live_match = (owner_of[:, :, None] == owner_ids[None, None, :]) & alive_slots[:, :, None]
    slot_of = jnp.min(jnp.where(live_match, slot_ids, slot_count), axis=1)
    attended_out, query_grad_out, partial_grads = fetch_attend(
        picks,
        owner_of,
        tile_lengths,
        slot_of,
        key_rows.reshape(blocks_here, TILE, model_width),
        value_rows.reshape(blocks_here, TILE, model_width),
        queries,
        cotangent,
    )
    fact_count = lax.axis_size("fact")
    span = model_width // fact_count
    pieces = lax.all_to_all(
        partial_grads.reshape(fact_count * owners, TILE, 2 * span),
        ("fact", "dim"), split_axis=0, concat_axis=0, tiled=True,
    )
    all_requests = lax.all_gather(requests.reshape(owners), "fact", tiled=True)
    key_grad_out, value_grad_out = sum_pieces(all_requests, pieces, blocks_here)
    return (
        attended_out,
        query_grad_out,
        key_grad_out,
        value_grad_out,
    )


def solution(mesh):
    in_specs = (
        P(("fact", "dim"), None),
        P("dim", None),
        P("dim", None),
        P(("fact", "dim"), None),
        P(("fact", "dim"), None),
        P(("fact", "dim")),
    )
    out_specs = (
        P(("fact", "dim"), None),
        P(("fact", "dim"), None),
        P("dim", "fact"),
        P("dim", "fact"),
    )
    return jax.shard_map(body, mesh=mesh, in_specs=in_specs, out_specs=out_specs, check_vma=False)
```

```python
import functools
import jax
import jax.numpy as jnp
from jax import lax
from jax.experimental import pallas as pl
from jax.experimental.pallas import tpu as pltpu
from jax.sharding import PartitionSpec as P

HEADS = 16
HEAD_DIM = 64
TILE = 128
NEG_FILL = -1e30
PAIR = 2 * HEAD_DIM


def _nt(a, b):
    return lax.dot_general(a, b, (((1,), (1,)), ((), ())), preferred_element_type=jnp.float32)


def _tn(a, b):
    return lax.dot_general(a, b, (((0,), (0,)), ((), ())), preferred_element_type=jnp.float32)


def _nn(a, b):
    return jnp.dot(a, b, preferred_element_type=jnp.float32)


def pair_attention(q, g, keys, values, alive, first):
    scale = HEAD_DIM ** (-0.5)
    outs = []
    for h in range(2):
        mine = first if h == 0 else jnp.logical_not(first)
        qh = jnp.where(mine, q, jnp.zeros_like(q))
        gh = jnp.where(mine, g, jnp.zeros_like(g))
        scores = _nt(qh, keys) * scale
        scores = jnp.where(alive, scores, NEG_FILL)
        row_max = jnp.max(scores, axis=-1, keepdims=True)
        expo = jnp.exp(scores - row_max)
        weights = expo / jnp.sum(expo, axis=-1, keepdims=True)
        weights_low = weights.astype(jnp.bfloat16)
        attended = _nn(weights_low, values)
        dweights = _nt(gh, values)
        row_delta = jnp.sum(weights * dweights, axis=-1, keepdims=True)
        dscores = (weights * (dweights - row_delta)).astype(jnp.bfloat16)
        query_grad = _nn(dscores, keys)
        key_grad = _tn(dscores, q)
        value_grad = _tn(weights_low, g)
        outs.append((attended, query_grad, key_grad, value_grad))
    pick = lambda i: jnp.where(first, outs[0][i], outs[1][i])
    return pick(0), pick(1) * scale, pick(2) * scale, pick(3)


def fetch_attend_kernel(pick_ref, owner_ref, length_ref, slot_ref, k_ref, v_ref, q_ref, g_ref,
                        att_ref, qg_ref, grad_ref,
                        stage, kbuf, vbuf, gbuf, gsend, send_sem, recv_sem, out_sem, *recv):
    owners = stage.shape[1]
    pairs = stage.shape[0]
    tiles = q_ref.shape[0] // TILE
    slots = kbuf.shape[0] // TILE
    me = lax.axis_index("dim")
    fact = lax.axis_index("fact")
    mesh = pl.DeviceIdType.MESH
    mine = pick_ref[me]
    for hp in range(pairs):
        cols = pl.ds(hp * PAIR, PAIR)
        recv[hp][me, 0] = k_ref[mine, :, cols]
        recv[hp][me, 1] = v_ref[mine, :, cols]
    barrier = pltpu.get_barrier_semaphore()
    for k in range(1, owners):
        pl.semaphore_signal(barrier, inc=1, device_id=(fact, lax.rem(me + k, owners)), device_id_type=mesh)
    for hp in range(pairs):
        cols = pl.ds(hp * PAIR, PAIR)
        for peer in range(owners):
            chosen = pick_ref[peer]
            stage[hp, peer, 0] = k_ref[chosen, :, cols]
            stage[hp, peer, 1] = v_ref[chosen, :, cols]
    pl.semaphore_wait(barrier, owners - 1)

    def remote(hp, k, src):
        dest = lax.rem(me + k, owners)
        return pltpu.make_async_remote_copy(
            src_ref=stage.at[hp, dest],
            dst_ref=recv[hp].at[src],
            send_sem=send_sem.at[hp, dest],
            recv_sem=recv_sem.at[hp, src],
            device_id=(fact, dest),
            device_id_type=mesh,
        )

    for hp in range(pairs):
        for k in range(1, owners):
            remote(hp, k, me).start()

    gbuf[:, slots] = jnp.zeros(gbuf.shape[:1] + gbuf.shape[2:], gbuf.dtype)
    lane = lax.broadcasted_iota(jnp.int32, (1, PAIR), 1)
    first = lane < HEAD_DIM
    key_pos = lax.broadcasted_iota(jnp.int32, (1, slots * TILE), 1)
    for hp in range(pairs):
        cols = pl.ds(hp * PAIR, PAIR)
        for k in range(1, owners):
            remote(hp, owners - k, lax.rem(me + k, owners)).wait_recv()
        for t in range(tiles):
            rows = pl.ds(t * TILE, TILE)
            for j in range(slots):
                owner = owner_ref[t, j]
                kbuf[pl.ds(j * TILE, TILE), :] = recv[hp][owner, 0]
                vbuf[pl.ds(j * TILE, TILE), :] = recv[hp][owner, 1]
            alive = key_pos < length_ref[t] * TILE
            attended, query_grad, key_grad, value_grad = pair_attention(
                q_ref[rows, cols], g_ref[rows, cols], kbuf[...], vbuf[...], alive, first
            )
            att_ref[rows, cols] = attended.astype(att_ref.dtype)
            qg_ref[rows, cols] = query_grad.astype(qg_ref.dtype)
            for j in range(slots):
                gbuf[t, j, :, :PAIR] = key_grad[j * TILE:(j + 1) * TILE]
                gbuf[t, j, :, PAIR:] = value_grad[j * TILE:(j + 1) * TILE]
        for owner in range(owners):
            total = gbuf[0, slot_ref[0, owner]]
            for t in range(1, tiles):
                total = total + gbuf[t, slot_ref[t, owner]]
            gsend[hp, owner] = total.astype(gsend.dtype)
        pltpu.make_async_copy(gsend.at[hp], grad_ref.at[hp], out_sem.at[hp]).start()
    for hp in range(pairs):
        for k in range(1, owners):
            remote(hp, k, me).wait_send()
        pltpu.make_async_copy(gsend.at[hp], grad_ref.at[hp], out_sem.at[hp]).wait()


def fetch_attend(picks, owner_of, tile_lengths, slot_of, key_blocks, value_blocks, queries, cotangent):
    _, _, width = key_blocks.shape
    owners = picks.shape[0]
    rows = queries.shape[0]
    slots = owner_of.shape[1]
    pairs = width // PAIR
    whole = pl.BlockSpec(memory_space=pltpu.VMEM)
    grid_spec = pltpu.PrefetchScalarGridSpec(
        num_scalar_prefetch=4,
        grid=(1,),
        in_specs=[whole] * 4,
        out_specs=[whole, whole, pl.BlockSpec(memory_space=pl.ANY)],
        scratch_shapes=[
            pltpu.VMEM((pairs, owners, 2, TILE, PAIR), jnp.bfloat16),
            pltpu.VMEM((slots * TILE, PAIR), jnp.bfloat16),
            pltpu.VMEM((slots * TILE, PAIR), jnp.bfloat16),
            pltpu.VMEM((rows // TILE, slots + 1, TILE, 2 * PAIR), jnp.float32),
            pltpu.VMEM((pairs, owners, TILE, 2 * PAIR), jnp.bfloat16),
            pltpu.SemaphoreType.DMA((pairs, owners)),
            pltpu.SemaphoreType.DMA((pairs, owners)),
            pltpu.SemaphoreType.DMA((pairs,)),
        ] + [pltpu.VMEM((owners, 2, TILE, PAIR), jnp.bfloat16) for _ in range(pairs)],
    )
    return pl.pallas_call(
        fetch_attend_kernel,
        grid_spec=grid_spec,
        out_shape=[
            jax.ShapeDtypeStruct((rows, width), jnp.bfloat16),
            jax.ShapeDtypeStruct((rows, width), jnp.bfloat16),
            jax.ShapeDtypeStruct((pairs, owners, TILE, 2 * PAIR), jnp.bfloat16),
        ],
        compiler_params=pltpu.CompilerParams(
            collective_id=0, has_side_effects=True, vmem_limit_bytes=60 * 1024 * 1024
        ),
    )(picks, owner_of, tile_lengths, slot_of, key_blocks, value_blocks, queries, cotangent)


def sum_kernel(req_ref, piece_ref, key_out, value_out, acc):
    step = pl.program_id(0)
    chunk = piece_ref.shape[0]
    span = key_out.shape[1]
    rows = piece_ref.shape[1]

    @pl.when(step == 0)
    def _():
        acc[...] = jnp.zeros_like(acc)

    spare = acc.shape[0] - 1
    for i in range(chunk):
        target = req_ref[step * chunk + i]
        target = jnp.where(target < 0, spare, jnp.minimum(target, spare))
        acc[target] = acc[target] + piece_ref[i].astype(jnp.float32)

    @pl.when(step == pl.num_programs(0) - 1)
    def _():
        for l in range(acc.shape[0] - 1):
            key_out[pl.ds(l * rows, rows), :] = acc[l, :, :span].astype(key_out.dtype)
            value_out[pl.ds(l * rows, rows), :] = acc[l, :, span:].astype(value_out.dtype)


def sum_pieces(all_requests, pieces, blocks):
    sources, rows, both = pieces.shape
    span = both // 2
    chunk = 32
    grid_spec = pltpu.PrefetchScalarGridSpec(
        num_scalar_prefetch=1,
        grid=(sources // chunk,),
        in_specs=[pl.BlockSpec((chunk, rows, both), lambda i, req: (i, 0, 0))],
        out_specs=[
            pl.BlockSpec((blocks * rows, span), lambda i, req: (0, 0)),
            pl.BlockSpec((blocks * rows, span), lambda i, req: (0, 0)),
        ],
        scratch_shapes=[pltpu.VMEM((blocks + 1, rows, both), jnp.float32)],
    )
    return pl.pallas_call(
        sum_kernel,
        grid_spec=grid_spec,
        out_shape=[
            jax.ShapeDtypeStruct((blocks * rows, span), jnp.bfloat16),
            jax.ShapeDtypeStruct((blocks * rows, span), jnp.bfloat16),
        ],
        compiler_params=pltpu.CompilerParams(dimension_semantics=("arbitrary",)),
    )(all_requests, pieces)


def body(queries, key_rows, value_rows, cotangent, block_lists, tile_lengths):
    owners = lax.axis_size("dim")
    tile_count = block_lists.shape[0]
    slot_count = block_lists.shape[1]
    blocks_here = key_rows.shape[0] // TILE
    model_width = key_rows.shape[1]
    alive_slots = jnp.arange(slot_count, dtype=jnp.int32)[None, :] < tile_lengths[:, None]
    owner_of = jnp.clip(block_lists // blocks_here, 0, owners - 1)
    local_of = block_lists % blocks_here
    owner_ids = jnp.arange(owners, dtype=jnp.int32)
    matched = (owner_of[:, :, None] == owner_ids[None, None, :]) & alive_slots[:, :, None]
    wanted = jnp.max(jnp.where(matched, local_of[:, :, None], -1), axis=(0, 1))
    requests = lax.all_to_all(
        wanted.reshape(owners, 1), "dim", split_axis=0, concat_axis=0, tiled=True
    )
    block_ids = jnp.arange(blocks_here, dtype=jnp.int32)[None, :]
    picks = jnp.clip(requests.reshape(owners), 0, blocks_here - 1)
    slot_ids = jnp.arange(slot_count, dtype=jnp.int32)[None, :, None]
    live_match = (owner_of[:, :, None] == owner_ids[None, None, :]) & alive_slots[:, :, None]
    slot_of = jnp.min(jnp.where(live_match, slot_ids, slot_count), axis=1)
    attended_out, query_grad_out, partial_grads = fetch_attend(
        picks,
        owner_of,
        tile_lengths,
        slot_of,
        key_rows.reshape(blocks_here, TILE, model_width),
        value_rows.reshape(blocks_here, TILE, model_width),
        queries,
        cotangent,
    )
    fact_count = lax.axis_size("fact")
    span = model_width // fact_count
    pieces = lax.all_to_all(
        partial_grads.reshape(fact_count * owners, TILE, 2 * span),
        ("fact", "dim"), split_axis=0, concat_axis=0, tiled=True,
    )
    all_requests = lax.all_gather(requests.reshape(owners), "fact", tiled=True)
    key_grad_out, value_grad_out = sum_pieces(all_requests, pieces, blocks_here)
    return (
        attended_out,
        query_grad_out,
        key_grad_out,
        value_grad_out,
    )


def solution(mesh):
    in_specs = (
        P(("fact", "dim"), None),
        P("dim", None),
        P("dim", None),
        P(("fact", "dim"), None),
        P(("fact", "dim"), None),
        P(("fact", "dim")),
    )
    out_specs = (
        P(("fact", "dim"), None),
        P(("fact", "dim"), None),
        P("dim", "fact"),
        P("dim", "fact"),
    )
    return jax.shard_map(body, mesh=mesh, in_specs=in_specs, out_specs=out_specs, check_vma=False)
```

```python
import functools
import jax
import jax.numpy as jnp
from jax import lax
from jax.experimental import pallas as pl
from jax.experimental.pallas import tpu as pltpu
from jax.sharding import PartitionSpec as P

HEADS = 16
HEAD_DIM = 64
TILE = 128
NEG_FILL = -1e30
PAIR = 2 * HEAD_DIM


def _nt(a, b):
    return lax.dot_general(a, b, (((1,), (1,)), ((), ())), preferred_element_type=jnp.float32)


def _tn(a, b):
    return lax.dot_general(a, b, (((0,), (0,)), ((), ())), preferred_element_type=jnp.float32)


def _nn(a, b):
    return jnp.dot(a, b, preferred_element_type=jnp.float32)


def pair_attention(q, g, keys, values, alive, first):
    scale = HEAD_DIM ** (-0.5)
    outs = []
    for h in range(2):
        mine = first if h == 0 else jnp.logical_not(first)
        qh = jnp.where(mine, q, jnp.zeros_like(q))
        gh = jnp.where(mine, g, jnp.zeros_like(g))
        scores = _nt(qh, keys) * scale
        scores = jnp.where(alive, scores, NEG_FILL)
        row_max = jnp.max(scores, axis=-1, keepdims=True)
        expo = jnp.exp(scores - row_max)
        weights = expo / jnp.sum(expo, axis=-1, keepdims=True)
        weights_low = weights.astype(jnp.bfloat16)
        attended = _nn(weights_low, values)
        dweights = _nt(gh, values)
        row_delta = jnp.sum(weights * dweights, axis=-1, keepdims=True)
        dscores = (weights * (dweights - row_delta)).astype(jnp.bfloat16)
        query_grad = _nn(dscores, keys)
        key_grad = _tn(dscores, q)
        value_grad = _tn(weights_low, g)
        outs.append((attended, query_grad, key_grad, value_grad))
    pick = lambda i: jnp.where(first, outs[0][i], outs[1][i])
    return pick(0), pick(1) * scale, pick(2) * scale, pick(3)


def fetch_attend_kernel(pick_ref, owner_ref, length_ref, slot_ref, k_ref, v_ref, q_ref, g_ref,
                        att_ref, qg_ref, grad_ref,
                        stage, kbuf, vbuf, gbuf, gsend, send_sem, recv_sem, out_sem, *recv):
    owners = stage.shape[1]
    pairs = stage.shape[0]
    tiles = q_ref.shape[0] // TILE
    slots = kbuf.shape[0] // TILE
    me = lax.axis_index("dim")
    fact = lax.axis_index("fact")
    mesh = pl.DeviceIdType.MESH
    mine = pick_ref[me]
    for hp in range(pairs):
        cols = pl.ds(hp * PAIR, PAIR)
        recv[hp][me, 0] = k_ref[mine, :, cols]
        recv[hp][me, 1] = v_ref[mine, :, cols]
    barrier = pltpu.get_barrier_semaphore()
    for k in range(1, owners):
        pl.semaphore_signal(barrier, inc=1, device_id=(fact, lax.rem(me + k, owners)), device_id_type=mesh)
    for hp in range(pairs):
        cols = pl.ds(hp * PAIR, PAIR)
        for peer in range(owners):
            chosen = pick_ref[peer]
            stage[hp, peer, 0] = k_ref[chosen, :, cols]
            stage[hp, peer, 1] = v_ref[chosen, :, cols]
    pl.semaphore_wait(barrier, owners - 1)

    def remote(hp, k, src):
        dest = lax.rem(me + k, owners)
        return pltpu.make_async_remote_copy(
            src_ref=stage.at[hp, dest],
            dst_ref=recv[hp].at[src],
            send_sem=send_sem.at[hp, dest],
            recv_sem=recv_sem.at[hp, src],
            device_id=(fact, dest),
            device_id_type=mesh,
        )

    for hp in range(pairs):
        for k in range(1, owners):
            remote(hp, k, me).start()

    gbuf[:, slots] = jnp.zeros(gbuf.shape[:1] + gbuf.shape[2:], gbuf.dtype)
    lane = lax.broadcasted_iota(jnp.int32, (1, PAIR), 1)
    first = lane < HEAD_DIM
    key_pos = lax.broadcasted_iota(jnp.int32, (1, slots * TILE), 1)
    for hp in range(pairs):
        cols = pl.ds(hp * PAIR, PAIR)
        for k in range(1, owners):
            remote(hp, owners - k, lax.rem(me + k, owners)).wait_recv()
        for t in range(tiles):
            rows = pl.ds(t * TILE, TILE)
            for j in range(slots):
                owner = owner_ref[t, j]
                kbuf[pl.ds(j * TILE, TILE), :] = recv[hp][owner, 0]
                vbuf[pl.ds(j * TILE, TILE), :] = recv[hp][owner, 1]
            alive = key_pos < length_ref[t] * TILE
            attended, query_grad, key_grad, value_grad = pair_attention(
                q_ref[rows, cols], g_ref[rows, cols], kbuf[...], vbuf[...], alive, first
            )
            att_ref[rows, cols] = attended.astype(att_ref.dtype)
            qg_ref[rows, cols] = query_grad.astype(qg_ref.dtype)
            for j in range(slots):
                gbuf[t, j, :, :PAIR] = key_grad[j * TILE:(j + 1) * TILE]
                gbuf[t, j, :, PAIR:] = value_grad[j * TILE:(j + 1) * TILE]
        for owner in range(owners):
            total = gbuf[0, slot_ref[0, owner]]
            for t in range(1, tiles):
                total = total + gbuf[t, slot_ref[t, owner]]
            gsend[hp, owner] = total.astype(gsend.dtype)
        pltpu.make_async_copy(gsend.at[hp], grad_ref.at[hp], out_sem.at[hp]).start()
    for hp in range(pairs):
        for k in range(1, owners):
            remote(hp, k, me).wait_send()
        pltpu.make_async_copy(gsend.at[hp], grad_ref.at[hp], out_sem.at[hp]).wait()


def fetch_attend(picks, owner_of, tile_lengths, slot_of, key_blocks, value_blocks, queries, cotangent):
    _, _, width = key_blocks.shape
    owners = picks.shape[0]
    rows = queries.shape[0]
    slots = owner_of.shape[1]
    pairs = width // PAIR
    whole = pl.BlockSpec(memory_space=pltpu.VMEM)
    grid_spec = pltpu.PrefetchScalarGridSpec(
        num_scalar_prefetch=4,
        grid=(1,),
        in_specs=[whole] * 4,
        out_specs=[whole, whole, pl.BlockSpec(memory_space=pl.ANY)],
        scratch_shapes=[
            pltpu.VMEM((pairs, owners, 2, TILE, PAIR), jnp.bfloat16),
            pltpu.VMEM((slots * TILE, PAIR), jnp.bfloat16),
            pltpu.VMEM((slots * TILE, PAIR), jnp.bfloat16),
            pltpu.VMEM((rows // TILE, slots + 1, TILE, 2 * PAIR), jnp.float32),
            pltpu.VMEM((pairs, owners, TILE, 2 * PAIR), jnp.bfloat16),
            pltpu.SemaphoreType.DMA((pairs, owners)),
            pltpu.SemaphoreType.DMA((pairs, owners)),
            pltpu.SemaphoreType.DMA((pairs,)),
        ] + [pltpu.VMEM((owners, 2, TILE, PAIR), jnp.bfloat16) for _ in range(pairs)],
    )
    return pl.pallas_call(
        fetch_attend_kernel,
        grid_spec=grid_spec,
        out_shape=[
            jax.ShapeDtypeStruct((rows, width), jnp.bfloat16),
            jax.ShapeDtypeStruct((rows, width), jnp.bfloat16),
            jax.ShapeDtypeStruct((pairs, owners, TILE, 2 * PAIR), jnp.bfloat16),
        ],
        compiler_params=pltpu.CompilerParams(
            collective_id=0, has_side_effects=True, vmem_limit_bytes=60 * 1024 * 1024
        ),
    )(picks, owner_of, tile_lengths, slot_of, key_blocks, value_blocks, queries, cotangent)


def sum_kernel(req_ref, piece_ref, key_out, value_out, acc):
    step = pl.program_id(0)
    chunk = piece_ref.shape[0]
    span = key_out.shape[1]
    rows = piece_ref.shape[1]

    @pl.when(step == 0)
    def _():
        acc[...] = jnp.zeros_like(acc)

    spare = acc.shape[0] - 1
    for i in range(chunk):
        target = req_ref[step * chunk + i]
        target = jnp.where(target < 0, spare, jnp.minimum(target, spare))
        acc[target] = acc[target] + piece_ref[i].astype(jnp.float32)

    @pl.when(step == pl.num_programs(0) - 1)
    def _():
        for l in range(acc.shape[0] - 1):
            key_out[pl.ds(l * rows, rows), :] = acc[l, :, :span].astype(key_out.dtype)
            value_out[pl.ds(l * rows, rows), :] = acc[l, :, span:].astype(value_out.dtype)


def sum_pieces(all_requests, pieces, blocks):
    sources, rows, both = pieces.shape
    span = both // 2
    chunk = 64
    grid_spec = pltpu.PrefetchScalarGridSpec(
        num_scalar_prefetch=1,
        grid=(sources // chunk,),
        in_specs=[pl.BlockSpec((chunk, rows, both), lambda i, req: (i, 0, 0))],
        out_specs=[
            pl.BlockSpec((blocks * rows, span), lambda i, req: (0, 0)),
            pl.BlockSpec((blocks * rows, span), lambda i, req: (0, 0)),
        ],
        scratch_shapes=[pltpu.VMEM((blocks + 1, rows, both), jnp.float32)],
    )
    return pl.pallas_call(
        sum_kernel,
        grid_spec=grid_spec,
        out_shape=[
            jax.ShapeDtypeStruct((blocks * rows, span), jnp.bfloat16),
            jax.ShapeDtypeStruct((blocks * rows, span), jnp.bfloat16),
        ],
        compiler_params=pltpu.CompilerParams(dimension_semantics=("arbitrary",)),
    )(all_requests, pieces)


def body(queries, key_rows, value_rows, cotangent, block_lists, tile_lengths):
    owners = lax.axis_size("dim")
    tile_count = block_lists.shape[0]
    slot_count = block_lists.shape[1]
    blocks_here = key_rows.shape[0] // TILE
    model_width = key_rows.shape[1]
    alive_slots = jnp.arange(slot_count, dtype=jnp.int32)[None, :] < tile_lengths[:, None]
    owner_of = jnp.clip(block_lists // blocks_here, 0, owners - 1)
    local_of = block_lists % blocks_here
    owner_ids = jnp.arange(owners, dtype=jnp.int32)
    matched = (owner_of[:, :, None] == owner_ids[None, None, :]) & alive_slots[:, :, None]
    wanted = jnp.max(jnp.where(matched, local_of[:, :, None], -1), axis=(0, 1))
    requests = lax.all_to_all(
        wanted.reshape(owners, 1), "dim", split_axis=0, concat_axis=0, tiled=True
    )
    block_ids = jnp.arange(blocks_here, dtype=jnp.int32)[None, :]
    picks = jnp.clip(requests.reshape(owners), 0, blocks_here - 1)
    slot_ids = jnp.arange(slot_count, dtype=jnp.int32)[None, :, None]
    live_match = (owner_of[:, :, None] == owner_ids[None, None, :]) & alive_slots[:, :, None]
    slot_of = jnp.min(jnp.where(live_match, slot_ids, slot_count), axis=1)
    attended_out, query_grad_out, partial_grads = fetch_attend(
        picks,
        owner_of,
        tile_lengths,
        slot_of,
        key_rows.reshape(blocks_here, TILE, model_width),
        value_rows.reshape(blocks_here, TILE, model_width),
        queries,
        cotangent,
    )
    fact_count = lax.axis_size("fact")
    span = model_width // fact_count
    pieces = lax.all_to_all(
        partial_grads.reshape(fact_count * owners, TILE, 2 * span),
        ("fact", "dim"), split_axis=0, concat_axis=0, tiled=True,
    )
    all_requests = lax.all_gather(requests.reshape(owners), "fact", tiled=True)
    key_grad_out, value_grad_out = sum_pieces(all_requests, pieces, blocks_here)
    return (
        attended_out,
        query_grad_out,
        key_grad_out,
        value_grad_out,
    )


def solution(mesh):
    in_specs = (
        P(("fact", "dim"), None),
        P("dim", None),
        P("dim", None),
        P(("fact", "dim"), None),
        P(("fact", "dim"), None),
        P(("fact", "dim")),
    )
    out_specs = (
        P(("fact", "dim"), None),
        P(("fact", "dim"), None),
        P("dim", "fact"),
        P("dim", "fact"),
    )
    return jax.shard_map(body, mesh=mesh, in_specs=in_specs, out_specs=out_specs, check_vma=False)
```
